256 devices in a mesh: bag: 16 (over x, y), seq: 16 (over z, core).
Axes of the slice: x: 4, y: 4, z: 8, core: 2. Of those that a mesh axis runs over, the one named last changes fastest.
Arguments:
- text_rows: bfloat16 [32768, 3072], P(('bag', 'seq')), may hold values from -6 to 6
- image_rows: bfloat16 [8192, 3072], P(('bag', 'seq')), may hold values from -6 to 6
- modulation: float32 [512, 2, 2, 3072], P('bag'), may hold values from -3 to 3
- head_weight: bfloat16 [2, 3072, 6144], P(None, None, 'seq'), may hold values from -0.109375 to 0.109375
- norm_gain: float32 [2, 2, 128], replicated, may hold values from 0.5 to 20
- store_down: bfloat16 [512, 2, 64, 3072], P('bag', None, 'seq'), may hold values from -0.109375 to 0.109375
- store_up: bfloat16 [512, 2, 64, 6144], P('bag', None, None, 'seq'), may hold values from -0.375 to 0.375
- store_row: int32 [512], replicated, may hold values from 0 to 511, as said below
- user_adapter: int32 [16, 16], replicated, may hold values from 0 to 511, as said below
- image_lengths: int32 [16, 16], P('bag'), may hold values from 1 to 128, 256 in all within a row
Outputs:
- text_out: bfloat16 [32768, 2048], P(('bag', 'seq'))
- image_out: bfloat16 [8192, 2048], P(('bag', 'seq'))
The draws below stay inside these ranges and needn't reach their ends.
Inputs may be any that keep to these rules, and one draw needn't show every extreme that they name: A permutation: adapter a is kept at row store_row[a] of store_down and store_up, whose owner is store_row[a] // 32. `user_adapter`: the 16 users of one bag have adapters kept by 16 different owners, so every owner keeps exactly one adapter of each bag.
All inputs are finite; a program needn't handle non-finite values.
Results may differ from the reference program's by a relative error of at most 0.04.
The reference program's roundings to bfloat16 on the way count: a program that leaves them out, or rounds other values in their place, can miss the bound.
Values may be sent and summed in bfloat16 or wider, within the bound.
A program may use at most 128 MiB of HBM per device.

```python
import math
import jax
import jax.numpy as jnp
import numpy as np
from jax import lax

D = 3072
HEAD_DIM = 128
HEADS = 16
RANK = 64
TEXT = 64
ADAPT_DEV = 32
USERS = 16
SEGMENTS = 32
TEXT_BAG = 2048
IMAGE_BAG = 512
ROWS_BAG = 2560
ADAPTERS = 512
N_BAG = 16


def adapter_layout(key):
    base_key = jax.random.fold_in(key, 11)
    perm_key, owner_key, slot_key = jax.random.split(base_key, 3)
    placement = jax.random.permutation(perm_key, ADAPTERS).astype(jnp.int32)
    inverse = jnp.argsort(placement).astype(jnp.int32)
    owner_keys = jax.random.split(owner_key, N_BAG)
    owner_lists = jax.vmap(lambda one_key: jax.random.permutation(one_key, N_BAG))(owner_keys)[:, :USERS].astype(jnp.int32)
    slot_pick = jax.random.randint(slot_key, (N_BAG, USERS), 0, ADAPT_DEV).astype(jnp.int32)
    store_rows = owner_lists * ADAPT_DEV + slot_pick
    return (placement, jnp.take(inverse, store_rows, axis=0).astype(jnp.int32))


def draw_store_row(key, part):
    return adapter_layout(key)[0]


def draw_user_adapter(key, part):
    return adapter_layout(key)[1]


def draw_norm_gain(key, part):
    value_key = jax.random.fold_in(jax.random.fold_in(key, 5), 0)
    return jnp.exp(jax.random.uniform(value_key, (2, 2, HEAD_DIM), jnp.float32, math.log(0.6), math.log(1.6))).astype(jnp.float32)


def block_levels(rng, dims, shards, least, high):
    gain, own = 1.0, jax.random.fold_in(rng, 6)
    for axis_at, blocks in shards:
        draws = jnp.exp(jax.random.uniform(jax.random.fold_in(own, axis_at), (blocks,), jnp.float32, least / len(shards), high / len(shards)))
        gain = gain * jnp.repeat(draws, dims[axis_at] // blocks).reshape([-1 if axis == axis_at else 1 for axis in range(len(dims))])
    return gain


def profile(number_of, total, reach, slope):
    portions = [(1 << 20) // math.isqrt(standing ** slope) + 1 for standing in range(2, number_of + 1)]
    spare, holding = total - reach - (number_of - 1), [1] * (number_of - 1)
    while spare > 0:
        free = [i for i in range(number_of - 1) if holding[i] < reach]
        whole, left = sum([portions[i] for i in free]), spare
        for i in free:
            more = min(reach - holding[i], max(1, left * portions[i] // whole), spare)
            holding[i] = holding[i] + more
            spare = spare - more
    return np.array([reach] + holding)


def uneven_parts(stream_key, number_of, total, bound, skew):
    if number_of == 2:
        one = jax.random.randint(stream_key, (), max(1, total - bound), min(bound, total - 1) + 1)
        return jnp.stack([one, total - one])
    tallies = jnp.asarray(profile(number_of, total, bound, skew), jnp.int32)
    couples = (number_of - 1) // 2
    donor, receiver = tallies[1:1 + 2 * couples:2], tallies[2:2 + 2 * couples:2]
    margin = jnp.minimum(donor - 1, bound - receiver)
    moved = jax.random.randint(jax.random.fold_in(stream_key, 1), (couples,), 0, 1 << 20) % (margin + 1)
    tallies = tallies.at[1:1 + 2 * couples:2].set(donor - moved).at[2:2 + 2 * couples:2].set(receiver + moved)
    return tallies[jax.random.permutation(jax.random.fold_in(stream_key, 2), number_of)]


def normal_values(key, shape, width, limit, shards=(), kind=jnp.bfloat16):
    gain = block_levels(key, shape, shards, -0.22, 0.18) if shards else 1.0
    entries = jax.random.normal(key, shape, jnp.float32) * width * gain
    return jnp.minimum(jnp.maximum(entries, -limit), limit).astype(kind)


def setup_inputs(seed: int = 0) -> dict:
    key_of = jax.random.split(jax.random.key(seed), 11)
    text_rows = normal_values(key_of[0], (N_BAG * TEXT_BAG, D), 1.0, 6.0, ((0, 256),))
    image_rows = normal_values(key_of[1], (N_BAG * IMAGE_BAG, D), 1.0, 6.0, ((0, 256),))
    modulation = normal_values(key_of[2], (N_BAG * SEGMENTS, 2, 2, D), 0.5, 3.0, ((0, 16),), jnp.float32)
    head_weight = normal_values(key_of[3], (2, D, 3 * HEADS * HEAD_DIM), D ** -0.5, 0.109375, ((2, 16),))
    norm_gain = draw_norm_gain(jax.random.fold_in(key_of[10], 71), 0)
    store_down = normal_values(key_of[5], (ADAPTERS, 2, RANK, D), D ** -0.5, 0.109375, ((0, 16), (2, 16)))
    store_up = normal_values(key_of[6], (ADAPTERS, 2, RANK, 3 * HEADS * HEAD_DIM), (4 * RANK) ** -0.5, 0.375, ((0, 16), (3, 16)))
    store_row = draw_store_row(jax.random.fold_in(key_of[10], 71), 0)
    user_adapter = draw_user_adapter(jax.random.fold_in(key_of[10], 71), 0)
    image_lengths = jax.vmap(lambda own: uneven_parts(own, USERS, IMAGE_BAG // 2, IMAGE_BAG // 4, 2))(jax.random.split(key_of[9], N_BAG)).reshape((N_BAG, USERS)).astype(jnp.int32)
    return {"text_rows": text_rows, "image_rows": image_rows, "modulation": modulation, "head_weight": head_weight, "norm_gain": norm_gain, "store_down": store_down, "store_up": store_up, "store_row": store_row, "user_adapter": user_adapter, "image_lengths": image_lengths}


def modulate(raw_rows, shifts, scales):
    values = raw_rows.astype(jnp.float32)
    centre = values - lax.optimization_barrier(jnp.mean(values, axis=-1, keepdims=True))
    spread = lax.optimization_barrier(jnp.mean(centre * centre, axis=-1, keepdims=True))
    normed = centre * lax.rsqrt(spread + 1e-06)
    return ((1.0 + scales) * normed + shifts).astype(jnp.bfloat16)

def head_normed(values, gain_row):
    spread = lax.optimization_barrier(jnp.mean(values * values, axis=-1, keepdims=True))
    return (values * lax.rsqrt(spread + 1e-06) * gain_row).astype(jnp.bfloat16)

def attend(queries, keys_all, values_all, seg_ids):
    row_total = queries.shape[0]
    block_rows = math.gcd(row_total, 1024)
    query_blocks = queries.reshape(row_total // block_rows, block_rows, queries.shape[1])
    seg_blocks = seg_ids.reshape(row_total // block_rows, block_rows)
    factor = 1.0 / math.sqrt(queries.shape[1])

    def one_block(block_pair):
        query_rows, query_segs = block_pair
        scores = jnp.dot(query_rows, keys_all.T, preferred_element_type=jnp.float32) * factor
        scores = jnp.where(query_segs[:, None] == seg_ids[None, :], scores, -1e+30)
        top_score = lax.optimization_barrier(jnp.max(scores, axis=1, keepdims=True))
        weights = jnp.exp(scores - top_score)
        prob_rows = (weights / lax.optimization_barrier(jnp.sum(weights, axis=1, keepdims=True))).astype(jnp.bfloat16)
        return jnp.dot(prob_rows, values_all, preferred_element_type=jnp.float32).astype(jnp.bfloat16)
    return lax.map(one_block, (query_blocks, seg_blocks)).reshape(row_total, values_all.shape[1])

def adapted(hidden, weight, down_users, up_users, user_ids, gain_pair):
    row_count = hidden.shape[0]
    user_count = down_users.shape[0]
    user_pick = user_ids[:, None] == jnp.arange(user_count, dtype=jnp.int32)[None, :]
    plain_part = jnp.dot(hidden, weight, preferred_element_type=jnp.float32)
    all_users = jnp.einsum('nd,urd->nur', hidden.astype(jnp.float32), down_users.astype(jnp.float32))
    ranks = lax.optimization_barrier(jnp.sum(all_users * user_pick.astype(jnp.float32)[:, :, None], axis=1)).astype(jnp.bfloat16)
    spread_ranks = (user_pick.astype(jnp.bfloat16)[:, :, None] * ranks[:, None, :]).reshape(row_count, -1)
    adjust = jnp.dot(spread_ranks, up_users.reshape(-1, weight.shape[1]), preferred_element_type=jnp.float32)
    mixed_cols = (plain_part + adjust).reshape(row_count, HEADS, 3, HEAD_DIM)
    query = head_normed(mixed_cols[:, :, 0], gain_pair[0])
    key_rows = head_normed(mixed_cols[:, :, 1], gain_pair[1])
    value_rows = mixed_cols[:, :, 2].astype(jnp.bfloat16)
    return (query, key_rows, value_rows)

def reference(text_rows, image_rows, modulation, head_weight, norm_gain, store_down, store_up, store_row, user_adapter, image_lengths):
    text_bags = text_rows.reshape(N_BAG, TEXT_BAG, D)
    image_bags = image_rows.reshape(N_BAG, IMAGE_BAG, D)
    mod_bags = modulation.reshape(N_BAG, SEGMENTS, 2, 2, D)
    text_segs = jnp.arange(TEXT_BAG, dtype=jnp.int32) // TEXT

    def one_bag(bag_items):
        text_bag, image_bag, mod_bag, adapters, lengths = bag_items
        seg_ends = jnp.cumsum(jnp.repeat(lengths, 2))
        image_segs = lax.optimization_barrier(jnp.sum((jnp.arange(IMAGE_BAG, dtype=jnp.int32)[:, None] >= seg_ends[None, :]).astype(jnp.int32), axis=1)).astype(jnp.int32)
        chosen = jnp.take(store_row, adapters, axis=0)
        down_sel = jnp.take(store_down, chosen, axis=0)
        up_sel = jnp.take(store_up, chosen, axis=0)
        text_hidden = modulate(text_bag, mod_bag[text_segs, 0, 0], mod_bag[text_segs, 0, 1])
        image_hidden = modulate(image_bag, mod_bag[image_segs, 1, 0], mod_bag[image_segs, 1, 1])
        text_parts = adapted(text_hidden, head_weight[0], down_sel[:, 0], up_sel[:, 0], text_segs // 2, norm_gain[0])
        image_parts = adapted(image_hidden, head_weight[1], down_sel[:, 1], up_sel[:, 1], image_segs // 2, norm_gain[1])
        joined = [jnp.transpose(jnp.concatenate([text_parts[which], image_parts[which]], axis=0), (1, 0, 2)) for which in range(3)]
        seg_all = jnp.concatenate([text_segs, image_segs], axis=0)

        def one_head(head_rows):
            return attend(head_rows[0], head_rows[1], head_rows[2], seg_all)
        outputs = lax.map(one_head, (joined[0], joined[1], joined[2]))
        outputs = jnp.transpose(outputs, (1, 0, 2)).reshape(ROWS_BAG, HEADS * HEAD_DIM)
        return (outputs[:TEXT_BAG], outputs[TEXT_BAG:])
    text_out, image_out = lax.map(one_bag, (text_bags, image_bags, mod_bags, user_adapter, image_lengths))
    return (text_out.reshape(N_BAG * TEXT_BAG, HEADS * HEAD_DIM), image_out.reshape(N_BAG * IMAGE_BAG, HEADS * HEAD_DIM))
```

```python
import functools
import math

import jax
import jax.numpy as jnp
from jax import lax
from jax.experimental import pallas as pl
from jax.experimental.pallas import tpu as pltpu
from jax.sharding import PartitionSpec as P

MESH = pl.DeviceIdType.MESH
BF16 = jnp.bfloat16
F32 = jnp.float32
I32 = jnp.int32
HEAD_DIM = 128
TEXT = 64
NEG = -1e30
NT = (((1,), (1,)), ((), ()))
TN = (((0,), (0,)), ((), ()))


def iota(shape, axis):
    return lax.broadcasted_iota(I32, shape, axis)


def normed(values):
    centre = values - jnp.mean(values, axis=-1, keepdims=True)
    spread = jnp.mean(centre * centre, axis=-1, keepdims=True)
    return centre * lax.rsqrt(spread + 1e-06)


def head_normed(values, gain_row):
    spread = jnp.mean(values * values, axis=-1, keepdims=True)
    return (values * lax.rsqrt(spread + 1e-06) * gain_row).astype(BF16)


def dot(a, b):
    return jnp.dot(a, b, preferred_element_type=F32)


def dot_g(a, b, dims):
    return lax.dot_general(a, b, dims, preferred_element_type=F32)


def kernel(
    bags,
    ring,
    store_size,
    user_adapter,
    store_row,
    image_lengths,
    text_in,
    image_in,
    mod_in,
    weight_in,
    gain_in,
    down_in,
    up_in,
    text_out,
    image_out,
    own,
    slot,
    ends,
    text_raw,
    image_raw,
    mod,
    weight,
    gain,
    down_store,
    up_store,
    down_send,
    up_send,
    down_recv,
    up_recv,
    down_fwd,
    text_down,
    image_scale,
    text_all,
    image_all,
    rank_all,
    image_rank,
    seg_row,
    seg_col,
    own_col,
    query_image,
    key_image,
    value_image,
    key_text,
    value_text,
    text_stage,
    image_stage,
    local_sem,
    bag_send,
    bag_recv,
    seq_send,
    seq_recv,
    ring_send,
    ring_recv,
    mate_send,
    mate_recv,
):
    seqs = 2 * ring
    half_ring = ring // 2
    users = seqs
    bag = lax.axis_index("bag")
    seq = lax.axis_index("seq")
    z, core = seq // 2, lax.rem(seq, 2)
    mate = z * 2 + 1 - core
    depth = text_raw.shape[1]
    text_rows = text_raw.shape[0]
    image_rows = image_raw.shape[0]
    image_bag = seqs * image_rows
    image_half = image_rows // 2
    factor = 1.0 / math.sqrt(HEAD_DIM)

    pairs = (
        (image_in, image_raw),
        (mod_in, mod),
        (text_in, text_raw),
        (down_in, down_store),
        (up_in, up_store),
        (gain_in, gain),
        (weight_in, weight),
    )
    loads = [
        pltpu.make_async_copy(src, dst, local_sem.at[i]) for i, (src, dst) in enumerate(pairs)
    ]
    for load in loads:
        load.start()

    barrier = pltpu.get_barrier_semaphore()

    @pl.loop(1, seqs)
    def _(j):
        pl.semaphore_signal(
            barrier, inc=1, device_id={"seq": lax.rem(seq + j, seqs)}, device_id_type=MESH
        )

    @pl.loop(1, bags)
    def _(j):
        pl.semaphore_signal(
            barrier, inc=1, device_id={"bag": lax.rem(bag + j, bags)}, device_id_type=MESH
        )

    def end_step(u, before):
        length = image_lengths[0, u]
        ends[2 * u] = before + length
        ends[2 * u + 1] = before + 2 * length
        own[u] = store_row[user_adapter[bag, u]] // store_size
        return before + 2 * length

    lax.fori_loop(0, users, end_step, jnp.int32(0))

    @pl.loop(0, bags)
    def _(b):
        def one(u, total):
            row = store_row[user_adapter[b, u]]
            return total + jnp.where(row // store_size == bag, lax.rem(row, store_size), 0)

        slot[b] = lax.fori_loop(0, users, one, jnp.int32(0))

    row_ids = iota((1, image_bag), 1)
    col_ids = iota((image_bag, HEAD_DIM), 0)

    def seg_step(j, pair):
        end = ends[j]
        return (
            pair[0] + (row_ids >= end).astype(I32),
            pair[1] + (col_ids >= end).astype(I32),
        )

    seg_r, seg_c = lax.fori_loop(
        0, 2 * users, seg_step, (jnp.zeros_like(row_ids), jnp.zeros_like(col_ids))
    )
    seg_row[...] = seg_r
    seg_col[...] = seg_c

    def own_step(u, pair):
        owner = own[u]
        return (
            pair[0] + jnp.where(seg_r // 2 == u, owner, 0),
            pair[1] + jnp.where(seg_c // 2 == u, owner, 0),
        )

    own_r, own_c = lax.fori_loop(
        0, users, own_step, (jnp.zeros_like(row_ids), jnp.zeros_like(col_ids))
    )
    own_col[...] = own_c

    loads[0].wait()
    loads[1].wait()

    @pl.loop(0, image_rows)
    def _(i):
        row = seq * image_rows + i
        seg = lax.fori_loop(
            0, 2 * users, lambda j, n: n + (row >= ends[j]).astype(I32), jnp.int32(0)
        )
        seg = jnp.minimum(seg, 2 * users - 1)
        image_scale[0, pl.ds(i, 1), :] = mod[seg, 1, 0:1, :]
        image_scale[1, pl.ds(i, 1), :] = mod[seg, 1, 1:2, :]

    for half in range(2):
        part = pl.ds(half * image_half, image_half)
        values = normed(image_raw[part, :].astype(F32))
        image_all[seq, half] = (
            (1.0 + image_scale[1, part, :]) * values + image_scale[0, part, :]
        ).astype(BF16)

    pl.semaphore_wait(barrier, seqs - 1 + bags - 1)

    blocks = (image_all, text_all)

    def slot_of(k, which):
        return lax.rem(z + k, ring) * 2 + which

    def ring_copy(st, d, k, half):
        chunk = blocks[st].at[slot_of(k, core), half]
        turn = ring - 1 if d == 0 else 1
        peer = lax.rem(z + (1 if d == 0 else ring - 1), ring) * 2 + core
        return pltpu.make_async_remote_copy(
            src_ref=chunk,
            dst_ref=chunk,
            send_sem=ring_send.at[st, d, k, half],
            recv_sem=ring_recv.at[st, lax.rem(k + turn, ring), half],
            device_id={"seq": peer},
            device_id_type=MESH,
        )

    def ring_arrival(st, k, half):
        chunk = blocks[st].at[slot_of(k, core), half]
        return pltpu.make_async_remote_copy(
            src_ref=chunk,
            dst_ref=chunk,
            send_sem=ring_send.at[st, 0, k, half],
            recv_sem=ring_recv.at[st, k, half],
            device_id={"seq": mate},
            device_id_type=MESH,
        )

    def mate_copy(st, k, half, which):
        chunk = blocks[st].at[slot_of(k, which), half]
        return pltpu.make_async_remote_copy(
            src_ref=chunk,
            dst_ref=chunk,
            send_sem=mate_send.at[st, k, half],
            recv_sem=mate_recv.at[st, k, half],
            device_id={"seq": mate},
            device_id_type=MESH,
        )

    def start_own(st, half):
        ring_copy(st, half, 0, half).start()
        ring_copy(st, 1 - half, 0, half).start()
        mate_copy(st, 0, half, core).start()

    def hop(st, h):
        for d, half in ((0, 0), (1, 1), (0, 1), (1, 0)):
            k = ring - h if d == 0 else h
            ring_arrival(st, k, half).wait_recv()
            if d == half:
                ring_copy(st, d, k, half).start()
            else:

                @pl.when(h < half_ring - 1)
                def _():
                    ring_copy(st, d, k, half).start()

            mate_copy(st, k, half, core).start()

    def last_hop(st):
        for half in range(2):
            ring_arrival(st, half_ring, half).wait_recv()
            mate_copy(st, half_ring, half, core).start()

    start_own(0, 0)
    start_own(0, 1)

    def down_copy(j):
        b = lax.rem(bag + j, bags)
        return pltpu.make_async_remote_copy(
            src_ref=down_send.at[b],
            dst_ref=down_recv.at[bag],
            send_sem=bag_send.at[0, j],
            recv_sem=bag_recv.at[0, j],
            device_id={"bag": b},
            device_id_type=MESH,
        )

    def up_copy(j):
        b = lax.rem(bag + j, bags)
        return pltpu.make_async_remote_copy(
            src_ref=up_send.at[b],
            dst_ref=up_recv.at[bag],
            send_sem=bag_send.at[1, j],
            recv_sem=bag_recv.at[1, j],
            device_id={"bag": b},
            device_id_type=MESH,
        )

    def bag_arrival(which, j):
        ref = (down_recv, up_recv)[which].at[lax.rem(bag + bags - j, bags)]
        return pltpu.make_async_remote_copy(
            src_ref=ref,
            dst_ref=ref,
            send_sem=bag_send.at[which, j],
            recv_sem=bag_recv.at[which, j],
            device_id={"bag": lax.rem(bag + j, bags)},
            device_id_type=MESH,
        )

    loads[3].wait()

    @pl.loop(1, bags)
    def _(j):
        b = lax.rem(bag + j, bags)
        down_send[b] = down_store[slot[b]]
        down_copy(j).start()

    down_recv[bag] = down_store[slot[bag]]

    loads[2].wait()
    for half in range(2):
        seg = 2 * seq + half
        shift = mod[seg, 0, 0:1, :]
        scale = 1.0 + mod[seg, 0, 1:2, :]

        @pl.loop(0, TEXT // 16)
        def _(i):
            values = normed(text_raw[pl.ds(half * TEXT + i * 16, 16), :].astype(F32))
            text_all[seq, half, pl.ds(i * 16, 16), :] = (scale * values + shift).astype(BF16)

        start_own(1, half)

    loads[4].wait()

    @pl.loop(1, bags)
    def _(j):
        b = lax.rem(bag + j, bags)
        up_send[b] = up_store[slot[b]]
        up_copy(j).start()

    up_recv[bag] = up_store[slot[bag]]

    hop(0, 1)

    def seq_copy(which, j, src, dst):
        return pltpu.make_async_remote_copy(
            src_ref=src,
            dst_ref=dst,
            send_sem=seq_send.at[which, j],
            recv_sem=seq_recv.at[which, j],
            device_id={"seq": lax.rem(seq + j, seqs)},
            device_id_type=MESH,
        )

    def ahead(j):
        return lax.rem(seq + j, seqs)

    def behind(j):
        return lax.rem(seq + seqs - j, seqs)

    def fwd_copy(j):
        return seq_copy(0, j, down_fwd.at[ahead(j)], text_down.at[seq])

    @pl.loop(1, bags)
    def _(j):
        bag_arrival(0, j).wait_recv()

    @pl.loop(1, seqs)
    def _(j):
        u = ahead(j)
        down_fwd[u] = down_recv[own[u], 0]
        fwd_copy(j).start()

    text_down[seq] = down_recv[own[seq], 0]

    @pl.loop(2, half_ring)
    def _(h):
        hop(0, h)

    last_hop(0)

    @pl.loop(1, seqs)
    def _(j):
        seq_copy(0, j, down_fwd.at[ahead(j)], text_down.at[behind(j)]).wait_recv()

    parts = 8 * seqs

    def rank_sums(downs, rows_lo, rows_hi):
        low = dot_g(downs, rows_lo, NT)
        high = dot_g(downs, rows_hi, NT)
        even = lax.rem(iota(low.shape, 0), 2) == 0
        mixed = jnp.where(even, low, high)
        total = mixed + pltpu.roll(mixed, low.shape[0] - 1, 0)
        return total, even

    downs = text_down[...].reshape(parts, depth // 2)
    total, even = rank_sums(
        downs,
        text_all[seq, :, :, : depth // 2].reshape(text_rows, depth // 2),
        text_all[seq, :, :, depth // 2 :].reshape(text_rows, depth // 2),
    )
    sums = jnp.where(even, total, 0.0).astype(BF16)
    take = (iota((parts // 2, parts), 1) == 2 * iota((parts // 2, parts), 0)).astype(BF16)
    rank_all[seq] = dot(take, sums).astype(BF16)

    def rank_copy(j):
        return seq_copy(1, j, rank_all.at[seq], rank_all.at[seq])

    @pl.loop(1, seqs)
    def _(j):
        rank_copy(j).start()

    @pl.loop(0, ring)
    def _(k):
        for half in range(2):
            mate_copy(0, k, half, 1 - core).wait_recv()

    downs = down_recv[:, 1].reshape(8 * bags, depth // 2)
    total, even = rank_sums(
        downs,
        image_all[:, :, :, : depth // 2].reshape(image_bag, depth // 2),
        image_all[:, :, :, depth // 2 :].reshape(image_bag, depth // 2),
    )
    mine = jnp.logical_and(even, iota(total.shape, 0) // 8 == own_r)
    sums = jnp.where(mine, total, 0.0).astype(BF16)
    at = iota((8, 8 * bags), 0)
    take = jnp.logical_and(lax.rem(iota(at.shape, 1), 8) == 2 * at, at < 4)
    image_rank[seq] = dot(take.astype(BF16), sums).astype(BF16)

    def image_rank_copy(j):
        return seq_copy(2, j, image_rank.at[seq], image_rank.at[seq])

    @pl.loop(1, seqs)
    def _(j):
        image_rank_copy(j).start()

    @pl.loop(1, bags)
    def _(j):
        bag_arrival(1, j).wait_recv()

    @pl.loop(1, seqs)
    def _(j):
        ref = image_rank.at[behind(j)]
        seq_copy(2, j, ref, ref).wait_recv()

    loads[5].wait()
    loads[6].wait()
    rank = parts // 2
    up_image = up_recv[:, 1].reshape(bags * rank, 3 * HEAD_DIM)
    lane = lax.rem(iota((parts, bags * rank), 1), rank)
    copies = (iota((parts, bags * rank), 0) == 8 * (lane // 4) + lax.rem(lane, 4)).astype(BF16)
    ranks = image_rank[...].reshape(parts, image_bag)
    for lot in range(2):
        lo, rows = lot * image_bag // 2, image_bag // 2
        spread = dot_g(ranks[:, lo : lo + rows], copies, TN)
        here = iota(spread.shape, 1) // rank == own_col[lo : lo + rows, 0:1]
        spread = jnp.where(here, spread, 0.0).astype(BF16)
        lot_rows = image_all[lot * seqs // 2 : (lot + 1) * seqs // 2].reshape(rows, depth)
        mixed = dot(lot_rows, weight[1]) + dot(spread, up_image)
        query_image[lo : lo + rows] = head_normed(mixed[:, :HEAD_DIM], gain[1, 0:1])
        key_image[lo : lo + rows] = head_normed(
            mixed[:, HEAD_DIM : 2 * HEAD_DIM], gain[1, 1:2]
        )
        value_image[lo : lo + rows] = mixed[:, 2 * HEAD_DIM :].astype(BF16)

    def text_out_copy(j):
        return pltpu.make_async_remote_copy(
            src_ref=text_stage.at[ahead(j)],
            dst_ref=text_out.at[seq],
            send_sem=seq_send.at[3, j],
            recv_sem=seq_recv.at[3, j],
            device_id={"seq": ahead(j)},
            device_id_type=MESH,
        )

    def image_out_copy(j):
        return pltpu.make_async_remote_copy(
            src_ref=image_stage.at[ahead(j)],
            dst_ref=image_out.at[seq],
            send_sem=seq_send.at[4, j],
            recv_sem=seq_recv.at[4, j],
            device_id={"seq": ahead(j)},
            device_id_type=MESH,
        )

    text_local = pltpu.make_async_copy(text_stage.at[seq], text_out.at[seq], local_sem.at[7])
    image_local = pltpu.make_async_copy(image_stage.at[seq], image_out.at[seq], local_sem.at[8])

    @pl.loop(1, half_ring)
    def _(h):
        hop(1, h)

    last_hop(1)

    @pl.loop(0, ring)
    def _(k):
        for half in range(2):
            mate_copy(1, k, half, 1 - core).wait_recv()

    @pl.loop(1, seqs)
    def _(j):
        ref = rank_all.at[behind(j)]
        seq_copy(1, j, ref, ref).wait_recv()

    @pl.loop(0, ring)
    def _(p):
        odd = lax.rem(p, 2)
        k = odd * (ring - (p + 1) // 2) + (1 - odd) * (p // 2)
        first = slot_of(k, 0)
        rows = text_all[pl.ds(first, 2)].reshape(2 * text_rows, depth)
        plain = dot(rows, weight[0])
        image_segs = seg_row[...]
        for which in range(2):
            u = first + which
            j = lax.rem(seq + seqs - u, seqs)

            adjust = dot_g(rank_all[u], up_recv[own[u], 0], TN)
            mixed = plain[which * text_rows : (which + 1) * text_rows] + adjust
            query = head_normed(mixed[:, :HEAD_DIM], gain[0, 0:1])
            key = head_normed(mixed[:, HEAD_DIM : 2 * HEAD_DIM], gain[0, 1:2])
            value = mixed[:, 2 * HEAD_DIM :].astype(BF16)
            key_text[u] = key
            value_text[u] = value
            near = dot_g(query, key, NT) * factor
            same = iota(near.shape, 0) // TEXT == iota(near.shape, 1) // TEXT
            near = jnp.where(same, near, NEG)
            far = dot_g(query, key_image[...], NT) * factor
            same = 2 * u + iota(far.shape, 0) // TEXT == image_segs
            far = jnp.where(same, far, NEG)
            top = jnp.maximum(
                jnp.max(near, axis=1, keepdims=True), jnp.max(far, axis=1, keepdims=True)
            )
            near = jnp.exp(near - top)
            far = jnp.exp(far - top)
            total = jnp.sum(near, axis=1, keepdims=True) + jnp.sum(far, axis=1, keepdims=True)
            result = dot((near / total).astype(BF16), value) + dot(
                (far / total).astype(BF16), value_image[...]
            )
            text_stage[u] = result.astype(BF16)

            @pl.when(j != 0)
            def _():
                text_out_copy(lax.rem(u + seqs - seq, seqs)).start()

            @pl.when(j == 0)
            def _():
                text_local.start()

    keys = key_text[...].reshape(seqs * text_rows, HEAD_DIM)
    values = value_text[...].reshape(seqs * text_rows, HEAD_DIM)

    @pl.loop(0, image_bag // HEAD_DIM)
    def _(lot):
        part = pl.ds(lot * HEAD_DIM, HEAD_DIM)
        query = query_image[part, :]
        segs = seg_col[part, 0:1]
        near = dot_g(query, key_image[...], NT) * factor
        near = jnp.where(segs == seg_row[...], near, NEG)
        far = dot_g(query, keys, NT) * factor
        far = jnp.where(segs == iota(far.shape, 1) // TEXT, far, NEG)
        top = jnp.maximum(
            jnp.max(near, axis=1, keepdims=True), jnp.max(far, axis=1, keepdims=True)
        )
        near = jnp.exp(near - top)
        far = jnp.exp(far - top)
        total = jnp.sum(near, axis=1, keepdims=True) + jnp.sum(far, axis=1, keepdims=True)
        result = dot((near / total).astype(BF16), value_image[...]) + dot(
            (far / total).astype(BF16), values
        )
        per = HEAD_DIM // image_rows
        image_stage[pl.ds(lot * per, per)] = result.astype(BF16).reshape(
            per, image_rows, HEAD_DIM
        )

    image_local.start()

    @pl.loop(1, seqs)
    def _(j):
        image_out_copy(j).start()

    text_local.wait()
    image_local.wait()

    @pl.loop(1, seqs)
    def _(j):
        seq_copy(3, j, text_stage.at[seq], text_out.at[behind(j)]).wait_recv()
        seq_copy(4, j, image_stage.at[seq], image_out.at[behind(j)]).wait_recv()
        fwd_copy(j).wait_send()
        rank_copy(j).wait_send()
        image_rank_copy(j).wait_send()
        text_out_copy(j).wait_send()
        image_out_copy(j).wait_send()

    @pl.loop(1, bags)
    def _(j):
        down_copy(j).wait_send()
        up_copy(j).wait_send()

    @pl.loop(0, ring)
    def _(k):
        for st in range(2):
            for half in range(2):
                mate_copy(st, k, half, core).wait_send()

    @pl.loop(0, half_ring - 1)
    def _(h):
        for st in range(2):
            for half in range(2):
                ring_copy(st, 0, lax.rem(ring - h, ring), half).wait_send()
                ring_copy(st, 1, h, half).wait_send()

    for st in range(2):
        ring_copy(st, 0, half_ring + 1, 0).wait_send()
        ring_copy(st, 1, half_ring - 1, 1).wait_send()


def body(
    bags,
    seqs,
    text_rows,
    image_rows,
    modulation,
    head_weight,
    norm_gain,
    store_down,
    store_up,
    store_row,
    user_adapter,
    image_lengths,
):
    ring = seqs // 2
    text_dev, depth = text_rows.shape
    image_dev = image_rows.shape[0]
    image_bag = image_dev * seqs
    store_size = store_down.shape[0]
    rank, width = store_up.shape[2:]
    heads = seqs * HEAD_DIM
    store_down = store_down.reshape(store_size, 2, 8, depth // 2)
    smem = pl.BlockSpec(memory_space=pltpu.SMEM)
    hbm = pl.BlockSpec(memory_space=pl.ANY)
    vmem = pltpu.VMEM
    dma = pltpu.SemaphoreType.DMA
    text_heads, image_heads = pl.pallas_call(
        functools.partial(kernel, bags, ring, store_size),
        out_shape=(
            jax.ShapeDtypeStruct((seqs, text_dev, HEAD_DIM), BF16),
            jax.ShapeDtypeStruct((seqs, image_dev, HEAD_DIM), BF16),
        ),
        in_specs=[smem] * 3 + [hbm] * 7,
        out_specs=(hbm, hbm),
        scratch_shapes=[
            pltpu.SMEM((seqs,), I32),
            pltpu.SMEM((bags,), I32),
            pltpu.SMEM((2 * seqs,), I32),
            vmem((text_dev, depth), BF16),
            vmem((image_dev, depth), BF16),
            vmem(modulation.shape, F32),
            vmem(head_weight.shape, BF16),
            vmem(norm_gain.shape, F32),
            vmem(store_down.shape, BF16),
            vmem(store_up.shape, BF16),
            vmem((bags, 2, 8, depth // 2), BF16),
            vmem((bags, 2, rank, width), BF16),
            vmem((bags, 2, 8, depth // 2), BF16),
            vmem((bags, 2, rank, width), BF16),
            vmem((seqs, 8, depth // 2), BF16),
            vmem((seqs, 8, depth // 2), BF16),
            vmem((2, image_dev, depth), F32),
            vmem((seqs, 2, text_dev // 2, depth), BF16),
            vmem((seqs, 2, image_dev // 2, depth), BF16),
            vmem((seqs, rank, text_dev), BF16),
            vmem((seqs, 8, image_bag), BF16),
            vmem((1, image_bag), I32),
            vmem((image_bag, HEAD_DIM), I32),
            vmem((image_bag, HEAD_DIM), I32),
            vmem((image_bag, HEAD_DIM), BF16),
            vmem((image_bag, HEAD_DIM), BF16),
            vmem((image_bag, HEAD_DIM), BF16),
            vmem((seqs, text_dev, HEAD_DIM), BF16),
            vmem((seqs, text_dev, HEAD_DIM), BF16),
            vmem((seqs, text_dev, HEAD_DIM), BF16),
            vmem((seqs, image_dev, HEAD_DIM), BF16),
            dma((9,)),
            dma((2, bags)),
            dma((2, bags)),
            dma((5, seqs)),
            dma((5, seqs)),
            dma((2, 2, ring, 2)),
            dma((2, ring, 2)),
            dma((2, ring, 2)),
            dma((2, ring, 2)),
        ],
        compiler_params=pltpu.CompilerParams(
            collective_id=0, has_side_effects=True, vmem_limit_bytes=58 * 2**20
        ),
    )(
        user_adapter,
        store_row,
        image_lengths,
        text_rows,
        image_rows,
        modulation,
        head_weight,
        norm_gain,
        store_down,
        store_up,
    )
    return (
        jnp.transpose(text_heads, (1, 0, 2)).reshape(text_dev, heads),
        jnp.transpose(image_heads, (1, 0, 2)).reshape(image_dev, heads),
    )


def solution(mesh):
    in_specs = (
        P(("bag", "seq"), None),
        P(("bag", "seq"), None),
        P("bag", None, None, None),
        P(None, None, "seq"),
        P(),
        P("bag", None, "seq", None),
        P("bag", None, None, "seq"),
        P(),
        P(),
        P("bag", None),
    )
    out_specs = (P(("bag", "seq"), None), P(("bag", "seq"), None))
    return jax.shard_map(
        functools.partial(body, mesh.shape["bag"], mesh.shape["seq"]),
        mesh=mesh,
        in_specs=in_specs,
        out_specs=out_specs,
        check_vma=False,
    )
```

```python
import functools
import math

import jax
import jax.numpy as jnp
from jax import lax
from jax.experimental import pallas as pl
from jax.experimental.pallas import tpu as pltpu
from jax.sharding import PartitionSpec as P

MESH = pl.DeviceIdType.MESH
BF16 = jnp.bfloat16
F32 = jnp.float32
I32 = jnp.int32
HEAD_DIM = 128
TEXT = 64
NEG = -1e30
NT = (((1,), (1,)), ((), ()))
TN = (((0,), (0,)), ((), ()))


def iota(shape, axis):
    return lax.broadcasted_iota(I32, shape, axis)


def normed(values):
    centre = values - jnp.mean(values, axis=-1, keepdims=True)
    spread = jnp.mean(centre * centre, axis=-1, keepdims=True)
    return centre * lax.rsqrt(spread + 1e-06)


def head_normed(values, gain_row):
    spread = jnp.mean(values * values, axis=-1, keepdims=True)
    return (values * lax.rsqrt(spread + 1e-06) * gain_row).astype(BF16)


def dot(a, b):
    return jnp.dot(a, b, preferred_element_type=F32)


def dot_g(a, b, dims):
    return lax.dot_general(a, b, dims, preferred_element_type=F32)


def kernel(
    bags,
    ring,
    store_size,
    user_adapter,
    store_row,
    image_lengths,
    text_in,
    image_in,
    mod_in,
    weight_in,
    gain_in,
    down_in,
    up_in,
    text_out,
    image_out,
    own,
    slot,
    ends,
    text_raw,
    image_raw,
    mod,
    weight,
    gain,
    down_store,
    up_store,
    down_send,
    up_send,
    down_recv,
    up_recv,
    down_fwd,
    text_down,
    image_scale,
    text_all,
    image_all,
    rank_all,
    image_rank,
    seg_row,
    seg_col,
    own_col,
    query_image,
    key_image,
    value_image,
    key_text,
    value_text,
    text_stage,
    image_stage,
    local_sem,
    bag_send,
    bag_recv,
    seq_send,
    seq_recv,
    ring_send,
    ring_recv,
    mate_send,
    mate_recv,
):
    seqs = 2 * ring
    half_ring = ring // 2
    users = seqs
    steps = [users >> i for i in range(users.bit_length())]
    store_bits = store_size.bit_length() - 1
    bag = lax.axis_index("bag")
    seq = lax.axis_index("seq")
    z, core = seq // 2, lax.rem(seq, 2)
    mate = z * 2 + 1 - core
    depth = text_raw.shape[1]
    text_rows = text_raw.shape[0]
    image_rows = image_raw.shape[0]
    image_bag = seqs * image_rows
    image_half = image_rows // 2
    factor = 1.0 / math.sqrt(HEAD_DIM)

    pairs = (
        (image_in, image_raw),
        (mod_in, mod),
        (text_in, text_raw),
        (down_in, down_store),
        (up_in, up_store),
        (gain_in, gain),
        (weight_in, weight),
    )
    loads = [
        pltpu.make_async_copy(src, dst, local_sem.at[i]) for i, (src, dst) in enumerate(pairs)
    ]
    for load in loads:
        load.start()

    barrier = pltpu.get_barrier_semaphore()

    @pl.loop(1, seqs)
    def _(j):
        pl.semaphore_signal(
            barrier, inc=1, device_id={"seq": lax.rem(seq + j, seqs)}, device_id_type=MESH
        )

    @pl.loop(1, bags)
    def _(j):
        pl.semaphore_signal(
            barrier, inc=1, device_id={"bag": lax.rem(bag + j, bags)}, device_id_type=MESH
        )

    before = jnp.int32(0)
    for u in range(users):
        length = image_lengths[0, u]
        ends[2 * u] = before + length
        before = before + 2 * length
        ends[2 * u + 1] = before

    loads[0].wait()
    loads[1].wait()

    @pl.loop(0, image_rows)
    def _(i):
        row = seq * image_rows + i
        seg = jnp.int32(0)
        for step in steps:
            seg = seg + jnp.where(row >= ends[seg + step - 1], step, 0)
        image_scale[0, pl.ds(i, 1), :] = mod[seg, 1, 0:1, :]
        image_scale[1, pl.ds(i, 1), :] = mod[seg, 1, 1:2, :]

    for half in range(2):
        part = pl.ds(half * image_half, image_half)
        values = normed(image_raw[part, :].astype(F32))
        image_all[seq, half] = (
            (1.0 + image_scale[1, part, :]) * values + image_scale[0, part, :]
        ).astype(BF16)

    pl.semaphore_wait(barrier, seqs - 1 + bags - 1)

    blocks = (image_all, text_all)

    def slot_of(k, which):
        return lax.rem(z + k, ring) * 2 + which

    def ring_copy(st, d, k, half):
        chunk = blocks[st].at[slot_of(k, core), half]
        turn = ring - 1 if d == 0 else 1
        peer = lax.rem(z + (1 if d == 0 else ring - 1), ring) * 2 + core
        return pltpu.make_async_remote_copy(
            src_ref=chunk,
            dst_ref=chunk,
            send_sem=ring_send.at[st, d, k, half],
            recv_sem=ring_recv.at[st, lax.rem(k + turn, ring), half],
            device_id={"seq": peer},
            device_id_type=MESH,
        )

    def ring_arrival(st, k, half):
        chunk = blocks[st].at[slot_of(k, core), half]
        return pltpu.make_async_remote_copy(
            src_ref=chunk,
            dst_ref=chunk,
            send_sem=ring_send.at[st, 0, k, half],
            recv_sem=ring_recv.at[st, k, half],
            device_id={"seq": mate},
            device_id_type=MESH,
        )

    def mate_copy(st, k, half, which):
        chunk = blocks[st].at[slot_of(k, which), half]
        return pltpu.make_async_remote_copy(
            src_ref=chunk,
            dst_ref=chunk,
            send_sem=mate_send.at[st, k, half],
            recv_sem=mate_recv.at[st, k, half],
            device_id={"seq": mate},
            device_id_type=MESH,
        )

    def start_own(st, half):
        ring_copy(st, half, 0, half).start()
        ring_copy(st, 1 - half, 0, half).start()
        mate_copy(st, 0, half, core).start()

    def hop(st, h):
        for d, half in ((0, 0), (1, 1), (0, 1), (1, 0)):
            k = ring - h if d == 0 else h
            ring_arrival(st, k, half).wait_recv()
            if d == half:
                ring_copy(st, d, k, half).start()
            else:

                @pl.when(h < half_ring - 1)
                def _():
                    ring_copy(st, d, k, half).start()

            mate_copy(st, k, half, core).start()

    def last_hop(st):
        for half in range(2):
            ring_arrival(st, half_ring, half).wait_recv()
            mate_copy(st, half_ring, half, core).start()

    start_own(0, 0)
    start_own(0, 1)

    def down_copy(j):
        b = lax.rem(bag + j, bags)
        return pltpu.make_async_remote_copy(
            src_ref=down_send.at[b],
            dst_ref=down_recv.at[bag],
            send_sem=bag_send.at[0, j],
            recv_sem=bag_recv.at[0, j],
            device_id={"bag": b},
            device_id_type=MESH,
        )

    def up_copy(j):
        b = lax.rem(bag + j, bags)
        return pltpu.make_async_remote_copy(
            src_ref=up_send.at[b],
            dst_ref=up_recv.at[bag],
            send_sem=bag_send.at[1, j],
            recv_sem=bag_recv.at[1, j],
            device_id={"bag": b},
            device_id_type=MESH,
        )

    def bag_arrival(which, j):
        ref = (down_recv, up_recv)[which].at[lax.rem(bag + bags - j, bags)]
        return pltpu.make_async_remote_copy(
            src_ref=ref,
            dst_ref=ref,
            send_sem=bag_send.at[which, j],
            recv_sem=bag_recv.at[which, j],
            device_id={"bag": lax.rem(bag + j, bags)},
            device_id_type=MESH,
        )

    @pl.loop(0, bags)
    def _(b):
        total = jnp.int32(0)
        for u in range(users):
            row = store_row[user_adapter[b, u]]
            total = total + jnp.where(row >> store_bits == bag, row & (store_size - 1), 0)
        slot[b] = total

    loads[3].wait()

    def put_down(ref, index, block):
        ref[index, :, 0:4, :] = block[:, :, : depth // 2]
        ref[index, :, 4:8, :] = block[:, :, depth // 2 :]

    @pl.loop(1, bags)
    def _(j):
        b = lax.rem(bag + j, bags)
        put_down(down_send, b, down_store[slot[b]])
        down_copy(j).start()

    put_down(down_recv, bag, down_store[slot[bag]])

    loads[2].wait()
    for half in range(2):
        seg = 2 * seq + half
        shift = mod[seg, 0, 0:1, :]
        scale = 1.0 + mod[seg, 0, 1:2, :]

        @pl.loop(0, TEXT // 16)
        def _(i):
            values = normed(text_raw[pl.ds(half * TEXT + i * 16, 16), :].astype(F32))
            text_all[seq, half, pl.ds(i * 16, 16), :] = (scale * values + shift).astype(BF16)

        start_own(1, half)

    loads[4].wait()

    @pl.loop(1, bags)
    def _(j):
        b = lax.rem(bag + j, bags)
        up_send[b] = up_store[slot[b]]
        up_copy(j).start()

    up_recv[bag] = up_store[slot[bag]]

    row_ids = iota((1, image_bag), 1)
    segs = jnp.zeros_like(row_ids)
    owners = jnp.zeros_like(row_ids)
    for j in range(2 * users):
        segs = segs + (row_ids >= ends[j]).astype(I32)
    for u in range(users):
        owner = store_row[user_adapter[bag, u]] >> store_bits
        own[u] = owner
        owners = owners + jnp.where(segs >> 1 == u, owner, 0)
    seg_row[...] = segs
    own_r = owners

    def as_column(row):
        wide = jnp.broadcast_to(row.astype(F32), (HEAD_DIM, image_bag))
        return jnp.transpose(wide).astype(I32)

    seg_col[...] = as_column(segs)
    own_col[...] = as_column(owners)

    hop(0, 1)

    def seq_copy(which, j, src, dst):
        return pltpu.make_async_remote_copy(
            src_ref=src,
            dst_ref=dst,
            send_sem=seq_send.at[which, j],
            recv_sem=seq_recv.at[which, j],
            device_id={"seq": lax.rem(seq + j, seqs)},
            device_id_type=MESH,
        )

    def ahead(j):
        return lax.rem(seq + j, seqs)

    def behind(j):
        return lax.rem(seq + seqs - j, seqs)

    def fwd_copy(j):
        return seq_copy(0, j, down_fwd.at[ahead(j)], text_down.at[seq])

    @pl.loop(1, bags)
    def _(j):
        bag_arrival(0, j).wait_recv()

    @pl.loop(1, seqs)
    def _(j):
        u = ahead(j)
        down_fwd[u] = down_recv[own[u], 0]
        fwd_copy(j).start()

    text_down[seq] = down_recv[own[seq], 0]

    @pl.loop(2, half_ring)
    def _(h):
        hop(0, h)

    last_hop(0)

    @pl.loop(1, seqs)
    def _(j):
        seq_copy(0, j, down_fwd.at[ahead(j)], text_down.at[behind(j)]).wait_recv()

    parts = 8 * seqs

    def rank_sums(downs, rows_lo, rows_hi):
        low = dot_g(downs, rows_lo, NT)
        high = dot_g(downs, rows_hi, NT)
        first = iota(low.shape, 0) & 7 < 4
        mixed = jnp.where(first, low, high)
        total = mixed + pltpu.roll(mixed, low.shape[0] - 4, 0)
        return total, first

    downs = text_down[...].reshape(parts, depth // 2)
    total, first = rank_sums(
        downs,
        text_all[seq, :, :, : depth // 2].reshape(text_rows, depth // 2),
        text_all[seq, :, :, depth // 2 :].reshape(text_rows, depth // 2),
    )
    sums = jnp.where(first, total, 0.0).astype(BF16)
    at = iota((parts // 2, parts), 0)
    take = (iota((parts // 2, parts), 1) == 8 * (at >> 2) + (at & 3)).astype(BF16)
    rank_all[seq] = dot(take, sums).astype(BF16)

    def rank_copy(j):
        return seq_copy(1, j, rank_all.at[seq], rank_all.at[seq])

    @pl.loop(1, seqs)
    def _(j):
        rank_copy(j).start()

    @pl.loop(0, ring)
    def _(k):
        for half in range(2):
            mate_copy(0, k, half, 1 - core).wait_recv()

    downs = down_recv[:, 1].reshape(8 * bags, depth // 2)
    total, first = rank_sums(
        downs,
        image_all[:, :, :, : depth // 2].reshape(image_bag, depth // 2),
        image_all[:, :, :, depth // 2 :].reshape(image_bag, depth // 2),
    )
    mine = jnp.logical_and(first, iota(total.shape, 0) >> 3 == own_r)
    sums = jnp.where(mine, total, 0.0).astype(BF16)
    at = iota((8, 8 * bags), 0)
    take = jnp.logical_and(iota(at.shape, 1) & 7 == at, at < 4)
    image_rank[seq] = dot(take.astype(BF16), sums).astype(BF16)

    def image_rank_copy(j):
        return seq_copy(2, j, image_rank.at[seq], image_rank.at[seq])

    @pl.loop(1, seqs)
    def _(j):
        image_rank_copy(j).start()

    @pl.loop(1, bags)
    def _(j):
        bag_arrival(1, j).wait_recv()

    @pl.loop(1, seqs)
    def _(j):
        ref = image_rank.at[behind(j)]
        seq_copy(2, j, ref, ref).wait_recv()

    loads[5].wait()
    loads[6].wait()
    rank = parts // 2
    up_image = up_recv[:, 1].reshape(bags * rank, 3 * HEAD_DIM)
    rank_bits = rank.bit_length() - 1
    lane = iota((parts, bags * rank), 1) & (rank - 1)
    copies = (iota((parts, bags * rank), 0) == 8 * (lane >> 2) + (lane & 3)).astype(BF16)
    ranks = image_rank[...].reshape(parts, image_bag)
    for lot in range(2):
        lo, rows = lot * image_bag // 2, image_bag // 2
        spread = dot_g(ranks[:, lo : lo + rows], copies, TN)
        here = iota(spread.shape, 1) >> rank_bits == own_col[lo : lo + rows, 0:1]
        spread = jnp.where(here, spread, 0.0).astype(BF16)
        lot_rows = image_all[lot * seqs // 2 : (lot + 1) * seqs // 2].reshape(rows, depth)
        mixed = dot(lot_rows, weight[1]) + dot(spread, up_image)
        query_image[lo : lo + rows] = head_normed(mixed[:, :HEAD_DIM], gain[1, 0:1])
        key_image[lo : lo + rows] = head_normed(
            mixed[:, HEAD_DIM : 2 * HEAD_DIM], gain[1, 1:2]
        )
        value_image[lo : lo + rows] = mixed[:, 2 * HEAD_DIM :].astype(BF16)

    def text_out_copy(j):
        return pltpu.make_async_remote_copy(
            src_ref=text_stage.at[ahead(j)],
            dst_ref=text_out.at[seq],
            send_sem=seq_send.at[3, j],
            recv_sem=seq_recv.at[3, j],
            device_id={"seq": ahead(j)},
            device_id_type=MESH,
        )

    def image_out_copy(j):
        return pltpu.make_async_remote_copy(
            src_ref=image_stage.at[ahead(j)],
            dst_ref=image_out.at[seq],
            send_sem=seq_send.at[4, j],
            recv_sem=seq_recv.at[4, j],
            device_id={"seq": ahead(j)},
            device_id_type=MESH,
        )

    text_local = pltpu.make_async_copy(text_stage.at[seq], text_out.at[seq], local_sem.at[7])
    image_local = pltpu.make_async_copy(image_stage.at[seq], image_out.at[seq], local_sem.at[8])

    @pl.loop(1, half_ring)
    def _(h):
        hop(1, h)

    last_hop(1)

    @pl.loop(0, ring)
    def _(k):
        for half in range(2):
            mate_copy(1, k, half, 1 - core).wait_recv()

    @pl.loop(1, seqs)
    def _(j):
        ref = rank_all.at[behind(j)]
        seq_copy(1, j, ref, ref).wait_recv()

    @pl.loop(0, ring)
    def _(p):
        odd = lax.rem(p, 2)
        k = odd * (ring - (p + 1) // 2) + (1 - odd) * (p // 2)
        first = slot_of(k, 0)
        rows = text_all[pl.ds(first, 2)].reshape(2 * text_rows, depth)
        plain = dot(rows, weight[0])
        image_segs = seg_row[...]
        for which in range(2):
            u = first + which
            j = lax.rem(seq + seqs - u, seqs)

            adjust = dot_g(rank_all[u], up_recv[own[u], 0], TN)
            mixed = plain[which * text_rows : (which + 1) * text_rows] + adjust
            query = head_normed(mixed[:, :HEAD_DIM], gain[0, 0:1])
            key = head_normed(mixed[:, HEAD_DIM : 2 * HEAD_DIM], gain[0, 1:2])
            value = mixed[:, 2 * HEAD_DIM :].astype(BF16)
            key_text[u] = key
            value_text[u] = value
            near = dot_g(query, key, NT) * factor
            same = iota(near.shape, 0) >> 6 == iota(near.shape, 1) >> 6
            near = jnp.where(same, near, NEG)
            far = dot_g(query, key_image[...], NT) * factor
            same = 2 * u + (iota(far.shape, 0) >> 6) == image_segs
            far = jnp.where(same, far, NEG)
            top = jnp.maximum(
                jnp.max(near, axis=1, keepdims=True), jnp.max(far, axis=1, keepdims=True)
            )
            near = jnp.exp(near - top)
            far = jnp.exp(far - top)
            total = jnp.sum(near, axis=1, keepdims=True) + jnp.sum(far, axis=1, keepdims=True)
            result = dot((near / total).astype(BF16), value) + dot(
                (far / total).astype(BF16), value_image[...]
            )
            text_stage[u] = result.astype(BF16)

            @pl.when(j != 0)
            def _():
                text_out_copy(lax.rem(u + seqs - seq, seqs)).start()

            @pl.when(j == 0)
            def _():
                text_local.start()

    keys = key_text[...].reshape(seqs * text_rows, HEAD_DIM)
    values = value_text[...].reshape(seqs * text_rows, HEAD_DIM)

    @pl.loop(0, image_bag // HEAD_DIM)
    def _(lot):
        part = pl.ds(lot * HEAD_DIM, HEAD_DIM)
        query = query_image[part, :]
        segs = seg_col[part, 0:1]
        near = dot_g(query, key_image[...], NT) * factor
        near = jnp.where(segs == seg_row[...], near, NEG)
        far = dot_g(query, keys, NT) * factor
        far = jnp.where(segs == iota(far.shape, 1) >> 6, far, NEG)
        top = jnp.maximum(
            jnp.max(near, axis=1, keepdims=True), jnp.max(far, axis=1, keepdims=True)
        )
        near = jnp.exp(near - top)
        far = jnp.exp(far - top)
        total = jnp.sum(near, axis=1, keepdims=True) + jnp.sum(far, axis=1, keepdims=True)
        result = dot((near / total).astype(BF16), value_image[...]) + dot(
            (far / total).astype(BF16), values
        )
        per = HEAD_DIM // image_rows
        image_stage[pl.ds(lot * per, per)] = result.astype(BF16).reshape(
            per, image_rows, HEAD_DIM
        )

    image_local.start()

    @pl.loop(1, seqs)
    def _(j):
        image_out_copy(j).start()

    text_local.wait()
    image_local.wait()

    @pl.loop(1, seqs)
    def _(j):
        seq_copy(3, j, text_stage.at[seq], text_out.at[behind(j)]).wait_recv()
        seq_copy(4, j, image_stage.at[seq], image_out.at[behind(j)]).wait_recv()
        fwd_copy(j).wait_send()
        rank_copy(j).wait_send()
        image_rank_copy(j).wait_send()
        text_out_copy(j).wait_send()
        image_out_copy(j).wait_send()

    @pl.loop(1, bags)
    def _(j):
        down_copy(j).wait_send()
        up_copy(j).wait_send()

    @pl.loop(0, ring)
    def _(k):
        for st in range(2):
            for half in range(2):
                mate_copy(st, k, half, core).wait_send()

    @pl.loop(0, half_ring - 1)
    def _(h):
        for st in range(2):
            for half in range(2):
                ring_copy(st, 0, lax.rem(ring - h, ring), half).wait_send()
                ring_copy(st, 1, h, half).wait_send()

    for st in range(2):
        ring_copy(st, 0, half_ring + 1, 0).wait_send()
        ring_copy(st, 1, half_ring - 1, 1).wait_send()


def body(
    bags,
    seqs,
    text_rows,
    image_rows,
    modulation,
    head_weight,
    norm_gain,
    store_down,
    store_up,
    store_row,
    user_adapter,
    image_lengths,
):
    ring = seqs // 2
    text_dev, depth = text_rows.shape
    image_dev = image_rows.shape[0]
    image_bag = image_dev * seqs
    store_size = store_down.shape[0]
    rank, width = store_up.shape[2:]
    heads = seqs * HEAD_DIM
    smem = pl.BlockSpec(memory_space=pltpu.SMEM)
    hbm = pl.BlockSpec(memory_space=pl.ANY)
    vmem = pltpu.VMEM
    dma = pltpu.SemaphoreType.DMA
    text_heads, image_heads = pl.pallas_call(
        functools.partial(kernel, bags, ring, store_size),
        out_shape=(
            jax.ShapeDtypeStruct((seqs, text_dev, HEAD_DIM), BF16),
            jax.ShapeDtypeStruct((seqs, image_dev, HEAD_DIM), BF16),
        ),
        in_specs=[smem] * 3 + [hbm] * 7,
        out_specs=(hbm, hbm),
        scratch_shapes=[
            pltpu.SMEM((seqs,), I32),
            pltpu.SMEM((bags,), I32),
            pltpu.SMEM((2 * seqs,), I32),
            vmem((text_dev, depth), BF16),
            vmem((image_dev, depth), BF16),
            vmem(modulation.shape, F32),
            vmem(head_weight.shape, BF16),
            vmem(norm_gain.shape, F32),
            vmem(store_down.shape, BF16),
            vmem(store_up.shape, BF16),
            vmem((bags, 2, 8, depth // 2), BF16),
            vmem((bags, 2, rank, width), BF16),
            vmem((bags, 2, 8, depth // 2), BF16),
            vmem((bags, 2, rank, width), BF16),
            vmem((seqs, 8, depth // 2), BF16),
            vmem((seqs, 8, depth // 2), BF16),
            vmem((2, image_dev, depth), F32),
            vmem((seqs, 2, text_dev // 2, depth), BF16),
            vmem((seqs, 2, image_dev // 2, depth), BF16),
            vmem((seqs, rank, text_dev), BF16),
            vmem((seqs, 8, image_bag), BF16),
            vmem((1, image_bag), I32),
            vmem((image_bag, HEAD_DIM), I32),
            vmem((image_bag, HEAD_DIM), I32),
            vmem((image_bag, HEAD_DIM), BF16),
            vmem((image_bag, HEAD_DIM), BF16),
            vmem((image_bag, HEAD_DIM), BF16),
            vmem((seqs, text_dev, HEAD_DIM), BF16),
            vmem((seqs, text_dev, HEAD_DIM), BF16),
            vmem((seqs, text_dev, HEAD_DIM), BF16),
            vmem((seqs, image_dev, HEAD_DIM), BF16),
            dma((9,)),
            dma((2, bags)),
            dma((2, bags)),
            dma((5, seqs)),
            dma((5, seqs)),
            dma((2, 2, ring, 2)),
            dma((2, ring, 2)),
            dma((2, ring, 2)),
            dma((2, ring, 2)),
        ],
        compiler_params=pltpu.CompilerParams(
            collective_id=0, has_side_effects=True, vmem_limit_bytes=58 * 2**20
        ),
    )(
        user_adapter,
        store_row,
        image_lengths,
        text_rows,
        image_rows,
        modulation,
        head_weight,
        norm_gain,
        store_down,
        store_up,
    )
    return (
        jnp.transpose(text_heads, (1, 0, 2)).reshape(text_dev, heads),
        jnp.transpose(image_heads, (1, 0, 2)).reshape(image_dev, heads),
    )


def solution(mesh):
    in_specs = (
        P(("bag", "seq"), None),
        P(("bag", "seq"), None),
        P("bag", None, None, None),
        P(None, None, "seq"),
        P(),
        P("bag", None, "seq", None),
        P("bag", None, None, "seq"),
        P(),
        P(),
        P("bag", None),
    )
    out_specs = (P(("bag", "seq"), None), P(("bag", "seq"), None))
    return jax.shard_map(
        functools.partial(body, mesh.shape["bag"], mesh.shape["seq"]),
        mesh=mesh,
        in_specs=in_specs,
        out_specs=out_specs,
        check_vma=False,
    )
```

```python
import functools
import math

import jax
import jax.numpy as jnp
from jax import lax
from jax.experimental import pallas as pl
from jax.experimental.pallas import tpu as pltpu
from jax.sharding import PartitionSpec as P

MESH = pl.DeviceIdType.MESH
BF16 = jnp.bfloat16
F32 = jnp.float32
I32 = jnp.int32
HEAD_DIM = 128
TEXT = 64
NEG = -1e30
NT = (((1,), (1,)), ((), ()))
TN = (((0,), (0,)), ((), ()))


def iota(shape, axis):
    return lax.broadcasted_iota(I32, shape, axis)


def normed(values):
    centre = values - jnp.mean(values, axis=-1, keepdims=True)
    spread = jnp.mean(centre * centre, axis=-1, keepdims=True)
    return centre * lax.rsqrt(spread + 1e-06)


def head_normed(values, gain_row):
    spread = jnp.mean(values * values, axis=-1, keepdims=True)
    return (values * lax.rsqrt(spread + 1e-06) * gain_row).astype(BF16)


def dot(a, b):
    return jnp.dot(a, b, preferred_element_type=F32)


def dot_g(a, b, dims):
    return lax.dot_general(a, b, dims, preferred_element_type=F32)


def kernel(
    bags,
    ring,
    store_size,
    user_adapter,
    store_row,
    image_lengths,
    text_in,
    image_in,
    mod_in,
    weight_in,
    gain_in,
    down_in,
    up_in,
    text_out,
    image_out,
    own,
    slot,
    ends,
    text_raw,
    image_raw,
    mod,
    weight,
    gain,
    down_store,
    up_store,
    down_send,
    up_send,
    down_recv,
    up_recv,
    down_fwd,
    text_down,
    image_scale,
    text_all,
    image_all,
    rank_all,
    image_rank,
    seg_row,
    seg_col,
    own_col,
    query_image,
    key_image,
    value_image,
    key_text,
    value_text,
    text_stage,
    image_stage,
    local_sem,
    bag_send,
    bag_recv,
    seq_send,
    seq_recv,
    ring_send,
    ring_recv,
    mate_send,
    mate_recv,
):
    seqs = 2 * ring
    half_ring = ring // 2
    users = seqs
    steps = [users >> i for i in range(users.bit_length())]
    store_bits = store_size.bit_length() - 1
    bag = lax.axis_index("bag")
    seq = lax.axis_index("seq")
    z, core = seq // 2, lax.rem(seq, 2)
    mate = z * 2 + 1 - core
    depth = text_raw.shape[1]
    text_rows = text_raw.shape[0]
    image_rows = image_raw.shape[0]
    image_bag = seqs * image_rows
    image_half = image_rows // 2
    factor = 1.0 / math.sqrt(HEAD_DIM)

    pairs = (
        (image_in, image_raw),
        (mod_in, mod),
        (text_in, text_raw),
        (down_in, down_store),
        (up_in, up_store),
        (gain_in, gain),
        (weight_in, weight),
    )
    loads = [
        pltpu.make_async_copy(src, dst, local_sem.at[i]) for i, (src, dst) in enumerate(pairs)
    ]
    for load in loads:
        load.start()

    barrier = pltpu.get_barrier_semaphore()

    @pl.loop(1, seqs)
    def _(j):
        pl.semaphore_signal(
            barrier, inc=1, device_id={"seq": lax.rem(seq + j, seqs)}, device_id_type=MESH
        )

    @pl.loop(1, bags)
    def _(j):
        pl.semaphore_signal(
            barrier, inc=1, device_id={"bag": lax.rem(bag + j, bags)}, device_id_type=MESH
        )

    before = jnp.int32(0)
    for u in range(users):
        length = image_lengths[0, u]
        ends[2 * u] = before + length
        before = before + 2 * length
        ends[2 * u + 1] = before

    loads[0].wait()
    loads[1].wait()

    @pl.loop(0, image_rows)
    def _(i):
        row = seq * image_rows + i
        seg = jnp.int32(0)
        for step in steps:
            seg = seg + jnp.where(row >= ends[seg + step - 1], step, 0)
        image_scale[0, pl.ds(i, 1), :] = mod[seg, 1, 0:1, :]
        image_scale[1, pl.ds(i, 1), :] = mod[seg, 1, 1:2, :]

    for half in range(2):
        part = pl.ds(half * image_half, image_half)
        values = normed(image_raw[part, :].astype(F32))
        image_all[seq, half] = (
            (1.0 + image_scale[1, part, :]) * values + image_scale[0, part, :]
        ).astype(BF16)

    pl.semaphore_wait(barrier, seqs - 1 + bags - 1)

    blocks = (image_all, text_all)

    def slot_of(k, which):
        return lax.rem(z + k, ring) * 2 + which

    def ring_copy(st, d, k, half):
        chunk = blocks[st].at[slot_of(k, core), half]
        turn = ring - 1 if d == 0 else 1
        peer = lax.rem(z + (1 if d == 0 else ring - 1), ring) * 2 + core
        return pltpu.make_async_remote_copy(
            src_ref=chunk,
            dst_ref=chunk,
            send_sem=ring_send.at[st, d, k, half],
            recv_sem=ring_recv.at[st, lax.rem(k + turn, ring), half],
            device_id={"seq": peer},
            device_id_type=MESH,
        )

    def ring_arrival(st, k, half):
        chunk = blocks[st].at[slot_of(k, core), half]
        return pltpu.make_async_remote_copy(
            src_ref=chunk,
            dst_ref=chunk,
            send_sem=ring_send.at[st, 0, k, half],
            recv_sem=ring_recv.at[st, k, half],
            device_id={"seq": mate},
            device_id_type=MESH,
        )

    def mate_copy(st, k, half, which):
        chunk = blocks[st].at[slot_of(k, which), half]
        return pltpu.make_async_remote_copy(
            src_ref=chunk,
            dst_ref=chunk,
            send_sem=mate_send.at[st, k, half],
            recv_sem=mate_recv.at[st, k, half],
            device_id={"seq": mate},
            device_id_type=MESH,
        )

    def start_own(st, half):
        ring_copy(st, half, 0, half).start()
        ring_copy(st, 1 - half, 0, half).start()
        mate_copy(st, 0, half, core).start()

    def hop(st, h):
        for d, half in ((0, 0), (1, 1), (0, 1), (1, 0)):
            k = ring - h if d == 0 else h
            ring_arrival(st, k, half).wait_recv()
            if d == half:
                ring_copy(st, d, k, half).start()
            elif h < half_ring - 1:
                ring_copy(st, d, k, half).start()

            mate_copy(st, k, half, core).start()

    def last_hop(st):
        for half in range(2):
            ring_arrival(st, half_ring, half).wait_recv()
            mate_copy(st, half_ring, half, core).start()

    start_own(0, 0)
    start_own(0, 1)

    def down_copy(j):
        b = lax.rem(bag + j, bags)
        return pltpu.make_async_remote_copy(
            src_ref=down_send.at[b],
            dst_ref=down_recv.at[bag],
            send_sem=bag_send.at[0, j],
            recv_sem=bag_recv.at[0, j],
            device_id={"bag": b},
            device_id_type=MESH,
        )

    def up_copy(j):
        b = lax.rem(bag + j, bags)
        return pltpu.make_async_remote_copy(
            src_ref=up_send.at[b],
            dst_ref=up_recv.at[bag],
            send_sem=bag_send.at[1, j],
            recv_sem=bag_recv.at[1, j],
            device_id={"bag": b},
            device_id_type=MESH,
        )

    def bag_arrival(which, j):
        ref = (down_recv, up_recv)[which].at[lax.rem(bag + bags - j, bags)]
        return pltpu.make_async_remote_copy(
            src_ref=ref,
            dst_ref=ref,
            send_sem=bag_send.at[which, j],
            recv_sem=bag_recv.at[which, j],
            device_id={"bag": lax.rem(bag + j, bags)},
            device_id_type=MESH,
        )

    @pl.loop(0, bags)
    def _(b):
        total = jnp.int32(0)
        for u in range(users):
            row = store_row[user_adapter[b, u]]
            total = total + jnp.where(row >> store_bits == bag, row & (store_size - 1), 0)
        slot[b] = total

    loads[3].wait()

    def put_down(ref, index, block):
        ref[index, :, 0:4, :] = block[:, :, : depth // 2]
        ref[index, :, 4:8, :] = block[:, :, depth // 2 :]

    @pl.loop(1, bags)
    def _(j):
        b = lax.rem(bag + j, bags)
        put_down(down_send, b, down_store[slot[b]])
        down_copy(j).start()

    put_down(down_recv, bag, down_store[slot[bag]])

    loads[2].wait()
    for half in range(2):
        seg = 2 * seq + half
        shift = mod[seg, 0, 0:1, :]
        scale = 1.0 + mod[seg, 0, 1:2, :]

        @pl.loop(0, TEXT // 16)
        def _(i):
            values = normed(text_raw[pl.ds(half * TEXT + i * 16, 16), :].astype(F32))
            text_all[seq, half, pl.ds(i * 16, 16), :] = (scale * values + shift).astype(BF16)

        start_own(1, half)

    loads[4].wait()

    @pl.loop(1, bags)
    def _(j):
        b = lax.rem(bag + j, bags)
        up_send[b] = up_store[slot[b]]
        up_copy(j).start()

    up_recv[bag] = up_store[slot[bag]]

    row_ids = iota((1, image_bag), 1)
    segs = jnp.zeros_like(row_ids)
    owners = jnp.zeros_like(row_ids)
    for j in range(2 * users):
        segs = segs + (row_ids >= ends[j]).astype(I32)
    for u in range(users):
        owner = store_row[user_adapter[bag, u]] >> store_bits
        own[u] = owner
        owners = owners + jnp.where(segs >> 1 == u, owner, 0)
    seg_row[...] = segs
    own_r = owners

    def as_column(row):
        wide = jnp.broadcast_to(row.astype(F32), (HEAD_DIM, image_bag))
        return jnp.transpose(wide).astype(I32)

    seg_col[...] = as_column(segs)
    own_col[...] = as_column(owners)

    hop(0, 1)

    def seq_copy(which, j, src, dst):
        return pltpu.make_async_remote_copy(
            src_ref=src,
            dst_ref=dst,
            send_sem=seq_send.at[which, j],
            recv_sem=seq_recv.at[which, j],
            device_id={"seq": lax.rem(seq + j, seqs)},
            device_id_type=MESH,
        )

    def ahead(j):
        return lax.rem(seq + j, seqs)

    def behind(j):
        return lax.rem(seq + seqs - j, seqs)

    def fwd_copy(j):
        return seq_copy(0, j, down_fwd.at[ahead(j)], text_down.at[seq])

    @pl.loop(1, bags)
    def _(j):
        bag_arrival(0, j).wait_recv()

    @pl.loop(1, seqs)
    def _(j):
        u = ahead(j)
        down_fwd[u] = down_recv[own[u], 0]
        fwd_copy(j).start()

    text_down[seq] = down_recv[own[seq], 0]

    for h in range(2, half_ring):
        hop(0, h)
    last_hop(0)

    hop(1, 1)

    @pl.loop(1, seqs)
    def _(j):
        seq_copy(0, j, down_fwd.at[ahead(j)], text_down.at[behind(j)]).wait_recv()

    parts = 8 * seqs

    def rank_sums(downs, rows_lo, rows_hi):
        low = dot_g(downs, rows_lo, NT)
        high = dot_g(downs, rows_hi, NT)
        first = iota(low.shape, 0) & 7 < 4
        mixed = jnp.where(first, low, high)
        total = mixed + pltpu.roll(mixed, low.shape[0] - 4, 0)
        return total, first

    downs = text_down[...].reshape(parts, depth // 2)
    total, first = rank_sums(
        downs,
        text_all[seq, :, :, : depth // 2].reshape(text_rows, depth // 2),
        text_all[seq, :, :, depth // 2 :].reshape(text_rows, depth // 2),
    )
    sums = jnp.where(first, total, 0.0).astype(BF16)
    at = iota((parts // 2, parts), 0)
    take = (iota((parts // 2, parts), 1) == 8 * (at >> 2) + (at & 3)).astype(BF16)
    rank_all[seq] = dot(take, sums).astype(BF16)

    rank_refs = (None, rank_all, image_rank)

    def core_copy(which, j):
        ref = rank_refs[which].at[seq]
        return pltpu.make_async_remote_copy(
            src_ref=ref,
            dst_ref=ref,
            send_sem=seq_send.at[which, j],
            recv_sem=seq_recv.at[which, j],
            device_id={"seq": slot_of(j, core)},
            device_id_type=MESH,
        )

    def core_arrival(which, j):
        ref = rank_refs[which].at[slot_of(ring - j, core)]
        return pltpu.make_async_remote_copy(
            src_ref=ref,
            dst_ref=ref,
            send_sem=seq_send.at[which, j],
            recv_sem=seq_recv.at[which, j],
            device_id={"seq": mate},
            device_id_type=MESH,
        )

    def pass_copy(which, k, side):
        ref = rank_refs[which].at[slot_of(k, side)]
        return pltpu.make_async_remote_copy(
            src_ref=ref,
            dst_ref=ref,
            send_sem=seq_send.at[which, ring + k],
            recv_sem=seq_recv.at[which, ring + k],
            device_id={"seq": mate},
            device_id_type=MESH,
        )

    def send_ranks(which):
        @pl.loop(1, ring)
        def _(j):
            core_copy(which, j).start()

        pass_copy(which, 0, core).start()

    def take_ranks(which):
        @pl.loop(1, ring)
        def _(j):
            core_arrival(which, j).wait_recv()
            pass_copy(which, ring - j, core).start()

        @pl.loop(0, ring)
        def _(k):
            pass_copy(which, k, 1 - core).wait_recv()

    send_ranks(1)

    @pl.loop(0, ring)
    def _(k):
        for half in range(2):
            mate_copy(0, k, half, 1 - core).wait_recv()

    downs = down_recv[:, 1].reshape(8 * bags, depth // 2)
    total, first = rank_sums(
        downs,
        image_all[:, :, :, : depth // 2].reshape(image_bag, depth // 2),
        image_all[:, :, :, depth // 2 :].reshape(image_bag, depth // 2),
    )
    mine = jnp.logical_and(first, iota(total.shape, 0) >> 3 == own_r)
    sums = jnp.where(mine, total, 0.0).astype(BF16)
    at = iota((8, 8 * bags), 0)
    take = jnp.logical_and(iota(at.shape, 1) & 7 == at, at < 4)
    image_rank[seq] = dot(take.astype(BF16), sums).astype(BF16)

    send_ranks(2)
    hop(1, 2)

    @pl.loop(1, bags)
    def _(j):
        bag_arrival(1, j).wait_recv()

    take_ranks(2)
    loads[5].wait()
    loads[6].wait()
    rank = parts // 2
    up_image = up_recv[:, 1].reshape(bags * rank, 3 * HEAD_DIM)
    rank_bits = rank.bit_length() - 1
    lane = iota((parts, bags * rank), 1) & (rank - 1)
    copies = (iota((parts, bags * rank), 0) == 8 * (lane >> 2) + (lane & 3)).astype(BF16)
    ranks = image_rank[...].reshape(parts, image_bag)
    for lot in range(2):
        lo, rows = lot * image_bag // 2, image_bag // 2
        spread = dot_g(ranks[:, lo : lo + rows], copies, TN)
        here = iota(spread.shape, 1) >> rank_bits == own_col[lo : lo + rows, 0:1]
        spread = jnp.where(here, spread, 0.0).astype(BF16)
        lot_rows = image_all[lot * seqs // 2 : (lot + 1) * seqs // 2].reshape(rows, depth)
        mixed = dot(lot_rows, weight[1]) + dot(spread, up_image)
        query_image[lo : lo + rows] = head_normed(mixed[:, :HEAD_DIM], gain[1, 0:1])
        key_image[lo : lo + rows] = head_normed(
            mixed[:, HEAD_DIM : 2 * HEAD_DIM], gain[1, 1:2]
        )
        value_image[lo : lo + rows] = mixed[:, 2 * HEAD_DIM :].astype(BF16)

    hop(1, 3)
    take_ranks(1)

    def text_out_copy(j):
        return pltpu.make_async_remote_copy(
            src_ref=text_stage.at[ahead(j)],
            dst_ref=text_out.at[seq],
            send_sem=seq_send.at[3, j],
            recv_sem=seq_recv.at[3, j],
            device_id={"seq": ahead(j)},
            device_id_type=MESH,
        )

    def image_out_copy(j):
        return pltpu.make_async_remote_copy(
            src_ref=image_stage.at[ahead(j)],
            dst_ref=image_out.at[seq],
            send_sem=seq_send.at[4, j],
            recv_sem=seq_recv.at[4, j],
            device_id={"seq": ahead(j)},
            device_id_type=MESH,
        )

    text_local = pltpu.make_async_copy(text_stage.at[seq], text_out.at[seq], local_sem.at[7])
    image_local = pltpu.make_async_copy(image_stage.at[seq], image_out.at[seq], local_sem.at[8])

    last_hop(1)

    @pl.loop(0, ring)
    def _(k):
        for half in range(2):
            mate_copy(1, k, half, 1 - core).wait_recv()

    @pl.loop(0, ring)
    def _(p):
        odd = lax.rem(p, 2)
        k = odd * (ring - (p + 1) // 2) + (1 - odd) * (p // 2)
        first = slot_of(k, 0)
        rows = text_all[pl.ds(first, 2)].reshape(2 * text_rows, depth)
        plain = dot(rows, weight[0])
        image_segs = seg_row[...]
        for which in range(2):
            u = first + which
            j = lax.rem(seq + seqs - u, seqs)

            adjust = dot_g(rank_all[u], up_recv[own[u], 0], TN)
            mixed = plain[which * text_rows : (which + 1) * text_rows] + adjust
            query = head_normed(mixed[:, :HEAD_DIM], gain[0, 0:1])
            key = head_normed(mixed[:, HEAD_DIM : 2 * HEAD_DIM], gain[0, 1:2])
            value = mixed[:, 2 * HEAD_DIM :].astype(BF16)
            key_text[u] = key
            value_text[u] = value
            near = dot_g(query, key, NT) * factor
            same = iota(near.shape, 0) >> 6 == iota(near.shape, 1) >> 6
            near = jnp.where(same, near, NEG)
            far = dot_g(query, key_image[...], NT) * factor
            same = 2 * u + (iota(far.shape, 0) >> 6) == image_segs
            far = jnp.where(same, far, NEG)
            top = jnp.maximum(
                jnp.max(near, axis=1, keepdims=True), jnp.max(far, axis=1, keepdims=True)
            )
            near = jnp.exp(near - top)
            far = jnp.exp(far - top)
            total = jnp.sum(near, axis=1, keepdims=True) + jnp.sum(far, axis=1, keepdims=True)
            result = dot((near / total).astype(BF16), value) + dot(
                (far / total).astype(BF16), value_image[...]
            )
            text_stage[u] = result.astype(BF16)

            @pl.when(j != 0)
            def _():
                text_out_copy(lax.rem(u + seqs - seq, seqs)).start()

            @pl.when(j == 0)
            def _():
                text_local.start()

    keys = key_text[...].reshape(seqs * text_rows, HEAD_DIM)
    values = value_text[...].reshape(seqs * text_rows, HEAD_DIM)

    @pl.loop(0, image_bag // HEAD_DIM)
    def _(lot):
        part = pl.ds(lot * HEAD_DIM, HEAD_DIM)
        query = query_image[part, :]
        segs = seg_col[part, 0:1]
        near = dot_g(query, key_image[...], NT) * factor
        near = jnp.where(segs == seg_row[...], near, NEG)
        far = dot_g(query, keys, NT) * factor
        far = jnp.where(segs == iota(far.shape, 1) >> 6, far, NEG)
        top = jnp.maximum(
            jnp.max(near, axis=1, keepdims=True), jnp.max(far, axis=1, keepdims=True)
        )
        near = jnp.exp(near - top)
        far = jnp.exp(far - top)
        total = jnp.sum(near, axis=1, keepdims=True) + jnp.sum(far, axis=1, keepdims=True)
        result = dot((near / total).astype(BF16), value_image[...]) + dot(
            (far / total).astype(BF16), values
        )
        per = HEAD_DIM // image_rows
        image_stage[pl.ds(lot * per, per)] = result.astype(BF16).reshape(
            per, image_rows, HEAD_DIM
        )

    image_local.start()

    @pl.loop(1, seqs)
    def _(j):
        image_out_copy(j).start()

    text_local.wait()
    image_local.wait()

    @pl.loop(1, seqs)
    def _(j):
        seq_copy(3, j, text_stage.at[seq], text_out.at[behind(j)]).wait_recv()
        seq_copy(4, j, image_stage.at[seq], image_out.at[behind(j)]).wait_recv()
        fwd_copy(j).wait_send()
        text_out_copy(j).wait_send()
        image_out_copy(j).wait_send()

    for which in (1, 2):

        @pl.loop(1, ring)
        def _(j):
            core_copy(which, j).wait_send()

        @pl.loop(0, ring)
        def _(k):
            pass_copy(which, k, core).wait_send()

    @pl.loop(1, bags)
    def _(j):
        down_copy(j).wait_send()
        up_copy(j).wait_send()

    @pl.loop(0, ring)
    def _(k):
        for st in range(2):
            for half in range(2):
                mate_copy(st, k, half, core).wait_send()

    @pl.loop(0, half_ring - 1)
    def _(h):
        for st in range(2):
            for half in range(2):
                ring_copy(st, 0, lax.rem(ring - h, ring), half).wait_send()
                ring_copy(st, 1, h, half).wait_send()

    for st in range(2):
        ring_copy(st, 0, half_ring + 1, 0).wait_send()
        ring_copy(st, 1, half_ring - 1, 1).wait_send()


def body(
    bags,
    seqs,
    text_rows,
    image_rows,
    modulation,
    head_weight,
    norm_gain,
    store_down,
    store_up,
    store_row,
    user_adapter,
    image_lengths,
):
    ring = seqs // 2
    text_dev, depth = text_rows.shape
    image_dev = image_rows.shape[0]
    image_bag = image_dev * seqs
    store_size = store_down.shape[0]
    rank, width = store_up.shape[2:]
    heads = seqs * HEAD_DIM
    smem = pl.BlockSpec(memory_space=pltpu.SMEM)
    hbm = pl.BlockSpec(memory_space=pl.ANY)
    vmem = pltpu.VMEM
    dma = pltpu.SemaphoreType.DMA
    text_heads, image_heads = pl.pallas_call(
        functools.partial(kernel, bags, ring, store_size),
        out_shape=(
            jax.ShapeDtypeStruct((seqs, text_dev, HEAD_DIM), BF16),
            jax.ShapeDtypeStruct((seqs, image_dev, HEAD_DIM), BF16),
        ),
        in_specs=[smem] * 3 + [hbm] * 7,
        out_specs=(hbm, hbm),
        scratch_shapes=[
            pltpu.SMEM((seqs,), I32),
            pltpu.SMEM((bags,), I32),
            pltpu.SMEM((2 * seqs,), I32),
            vmem((text_dev, depth), BF16),
            vmem((image_dev, depth), BF16),
            vmem(modulation.shape, F32),
            vmem(head_weight.shape, BF16),
            vmem(norm_gain.shape, F32),
            vmem(store_down.shape, BF16),
            vmem(store_up.shape, BF16),
            vmem((bags, 2, 8, depth // 2), BF16),
            vmem((bags, 2, rank, width), BF16),
            vmem((bags, 2, 8, depth // 2), BF16),
            vmem((bags, 2, rank, width), BF16),
            vmem((seqs, 8, depth // 2), BF16),
            vmem((seqs, 8, depth // 2), BF16),
            vmem((2, image_dev, depth), F32),
            vmem((seqs, 2, text_dev // 2, depth), BF16),
            vmem((seqs, 2, image_dev // 2, depth), BF16),
            vmem((seqs, rank, text_dev), BF16),
            vmem((seqs, 8, image_bag), BF16),
            vmem((1, image_bag), I32),
            vmem((image_bag, HEAD_DIM), I32),
            vmem((image_bag, HEAD_DIM), I32),
            vmem((image_bag, HEAD_DIM), BF16),
            vmem((image_bag, HEAD_DIM), BF16),
            vmem((image_bag, HEAD_DIM), BF16),
            vmem((seqs, text_dev, HEAD_DIM), BF16),
            vmem((seqs, text_dev, HEAD_DIM), BF16),
            vmem((seqs, text_dev, HEAD_DIM), BF16),
            vmem((seqs, image_dev, HEAD_DIM), BF16),
            dma((9,)),
            dma((2, bags)),
            dma((2, bags)),
            dma((5, seqs)),
            dma((5, seqs)),
            dma((2, 2, ring, 2)),
            dma((2, ring, 2)),
            dma((2, ring, 2)),
            dma((2, ring, 2)),
        ],
        compiler_params=pltpu.CompilerParams(
            collective_id=0, has_side_effects=True, vmem_limit_bytes=58 * 2**20
        ),
    )(
        user_adapter,
        store_row,
        image_lengths,
        text_rows,
        image_rows,
        modulation,
        head_weight,
        norm_gain,
        store_down,
        store_up,
    )
    return (
        jnp.transpose(text_heads, (1, 0, 2)).reshape(text_dev, heads),
        jnp.transpose(image_heads, (1, 0, 2)).reshape(image_dev, heads),
    )


def solution(mesh):
    in_specs = (
        P(("bag", "seq"), None),
        P(("bag", "seq"), None),
        P("bag", None, None, None),
        P(None, None, "seq"),
        P(),
        P("bag", None, "seq", None),
        P("bag", None, None, "seq"),
        P(),
        P(),
        P("bag", None),
    )
    out_specs = (P(("bag", "seq"), None), P(("bag", "seq"), None))
    return jax.shard_map(
        functools.partial(body, mesh.shape["bag"], mesh.shape["seq"]),
        mesh=mesh,
        in_specs=in_specs,
        out_specs=out_specs,
        check_vma=False,
    )
```

```python
import functools
import math

import jax
import jax.numpy as jnp
from jax import lax
from jax.experimental import pallas as pl
from jax.experimental.pallas import tpu as pltpu
from jax.sharding import PartitionSpec as P

MESH = pl.DeviceIdType.MESH
BF16 = jnp.bfloat16
F32 = jnp.float32
I32 = jnp.int32
HEAD_DIM = 128
TEXT = 64
NEG = -1e30
NT = (((1,), (1,)), ((), ()))
TN = (((0,), (0,)), ((), ()))


def iota(shape, axis):
    return lax.broadcasted_iota(I32, shape, axis)


def normed(values):
    centre = values - jnp.mean(values, axis=-1, keepdims=True)
    spread = jnp.mean(centre * centre, axis=-1, keepdims=True)
    return centre * lax.rsqrt(spread + 1e-06)


def head_normed(values, gain_row):
    spread = jnp.mean(values * values, axis=-1, keepdims=True)
    return (values * lax.rsqrt(spread + 1e-06) * gain_row).astype(BF16)


def dot(a, b):
    return jnp.dot(a, b, preferred_element_type=F32)


def dot_g(a, b, dims):
    return lax.dot_general(a, b, dims, preferred_element_type=F32)


def kernel(
    bags,
    ring,
    store_size,
    user_adapter,
    store_row,
    image_lengths,
    text_in,
    image_in,
    mod_in,
    weight_in,
    gain_in,
    down_in,
    up_in,
    text_out,
    image_out,
    own,
    slot,
    ends,
    text_raw,
    image_raw,
    mod,
    weight,
    gain,
    down_store,
    up_store,
    down_send,
    up_send,
    down_recv,
    up_recv,
    down_fwd,
    text_down,
    image_scale,
    text_all,
    image_all,
    rank_all,
    image_rank,
    seg_row,
    seg_col,
    own_col,
    query_image,
    key_image,
    value_image,
    key_text,
    value_text,
    text_stage,
    image_stage,
    local_sem,
    bag_send,
    bag_recv,
    seq_send,
    seq_recv,
    ring_send,
    ring_recv,
    mate_send,
    mate_recv,
):
    seqs = 2 * ring
    half_ring = ring // 2
    users = seqs
    steps = [users >> i for i in range(users.bit_length())]
    store_bits = store_size.bit_length() - 1
    bag = lax.axis_index("bag")
    seq = lax.axis_index("seq")
    z, core = seq // 2, lax.rem(seq, 2)
    mate = z * 2 + 1 - core
    depth = text_raw.shape[1]
    text_rows = text_raw.shape[0]
    image_rows = image_raw.shape[0]
    image_bag = seqs * image_rows
    image_half = image_rows // 2
    factor = 1.0 / math.sqrt(HEAD_DIM)

    pairs = (
        (image_in, image_raw),
        (mod_in, mod),
        (text_in, text_raw),
        (down_in, down_store),
        (up_in, up_store),
        (gain_in, gain),
        (weight_in, weight),
    )
    loads = [
        pltpu.make_async_copy(src, dst, local_sem.at[i]) for i, (src, dst) in enumerate(pairs)
    ]
    for load in loads:
        load.start()

    barrier = pltpu.get_barrier_semaphore()

    @pl.loop(1, seqs)
    def _(j):
        pl.semaphore_signal(
            barrier, inc=1, device_id={"seq": lax.rem(seq + j, seqs)}, device_id_type=MESH
        )

    @pl.loop(1, bags)
    def _(j):
        pl.semaphore_signal(
            barrier, inc=1, device_id={"bag": lax.rem(bag + j, bags)}, device_id_type=MESH
        )

    before = jnp.int32(0)
    for u in range(users):
        length = image_lengths[0, u]
        ends[2 * u] = before + length
        before = before + 2 * length
        ends[2 * u + 1] = before

    loads[0].wait()
    loads[1].wait()

    @pl.loop(0, image_rows)
    def _(i):
        row = seq * image_rows + i
        seg = jnp.int32(0)
        for step in steps:
            seg = seg + jnp.where(row >= ends[seg + step - 1], step, 0)
        image_scale[0, pl.ds(i, 1), :] = mod[seg, 1, 0:1, :]
        image_scale[1, pl.ds(i, 1), :] = mod[seg, 1, 1:2, :]

    for half in range(2):
        part = pl.ds(half * image_half, image_half)
        values = normed(image_raw[part, :].astype(F32))
        image_all[seq, half] = (
            (1.0 + image_scale[1, part, :]) * values + image_scale[0, part, :]
        ).astype(BF16)

    pl.semaphore_wait(barrier, seqs - 1 + bags - 1)

    blocks = (image_all, text_all)

    def slot_of(k, which):
        return lax.rem(z + k, ring) * 2 + which

    def ring_copy(st, d, k, half):
        chunk = blocks[st].at[slot_of(k, core), half]
        turn = ring - 1 if d == 0 else 1
        peer = lax.rem(z + (1 if d == 0 else ring - 1), ring) * 2 + core
        return pltpu.make_async_remote_copy(
            src_ref=chunk,
            dst_ref=chunk,
            send_sem=ring_send.at[st, d, k, half],
            recv_sem=ring_recv.at[st, lax.rem(k + turn, ring), half],
            device_id={"seq": peer},
            device_id_type=MESH,
        )

    def ring_arrival(st, k, half):
        chunk = blocks[st].at[slot_of(k, core), half]
        return pltpu.make_async_remote_copy(
            src_ref=chunk,
            dst_ref=chunk,
            send_sem=ring_send.at[st, 0, k, half],
            recv_sem=ring_recv.at[st, k, half],
            device_id={"seq": mate},
            device_id_type=MESH,
        )

    def mate_copy(st, k, half, which):
        chunk = blocks[st].at[slot_of(k, which), half]
        return pltpu.make_async_remote_copy(
            src_ref=chunk,
            dst_ref=chunk,
            send_sem=mate_send.at[st, k, half],
            recv_sem=mate_recv.at[st, k, half],
            device_id={"seq": mate},
            device_id_type=MESH,
        )

    def start_own(st, half):
        ring_copy(st, half, 0, half).start()
        ring_copy(st, 1 - half, 0, half).start()
        mate_copy(st, 0, half, core).start()

    def hop(st, h):
        for d, half in ((0, 0), (1, 1), (0, 1), (1, 0)):
            k = ring - h if d == 0 else h
            ring_arrival(st, k, half).wait_recv()
            if d == half:
                ring_copy(st, d, k, half).start()
            elif h < half_ring - 1:
                ring_copy(st, d, k, half).start()

            mate_copy(st, k, half, core).start()

    def last_hop(st):
        for half in range(2):
            ring_arrival(st, half_ring, half).wait_recv()
            mate_copy(st, half_ring, half, core).start()

    start_own(0, 0)
    start_own(0, 1)

    def down_copy(j):
        b = lax.rem(bag + j, bags)
        return pltpu.make_async_remote_copy(
            src_ref=down_send.at[b],
            dst_ref=down_recv.at[bag],
            send_sem=bag_send.at[0, j],
            recv_sem=bag_recv.at[0, j],
            device_id={"bag": b},
            device_id_type=MESH,
        )

    def up_copy(j):
        b = lax.rem(bag + j, bags)
        return pltpu.make_async_remote_copy(
            src_ref=up_send.at[b],
            dst_ref=up_recv.at[bag],
            send_sem=bag_send.at[1, j],
            recv_sem=bag_recv.at[1, j],
            device_id={"bag": b},
            device_id_type=MESH,
        )

    def bag_arrival(which, j):
        ref = (down_recv, up_recv)[which].at[lax.rem(bag + bags - j, bags)]
        return pltpu.make_async_remote_copy(
            src_ref=ref,
            dst_ref=ref,
            send_sem=bag_send.at[which, j],
            recv_sem=bag_recv.at[which, j],
            device_id={"bag": lax.rem(bag + j, bags)},
            device_id_type=MESH,
        )

    @pl.loop(0, bags)
    def _(b):
        total = jnp.int32(0)
        for u in range(users):
            row = store_row[user_adapter[b, u]]
            total = total + jnp.where(row >> store_bits == bag, row & (store_size - 1), 0)
        slot[b] = total

    loads[3].wait()

    def put_down(ref, index, block):
        ref[index, :, 0:4, :] = block[:, :, : depth // 2]
        ref[index, :, 4:8, :] = block[:, :, depth // 2 :]

    @pl.loop(1, bags)
    def _(j):
        b = lax.rem(bag + j, bags)
        put_down(down_send, b, down_store[slot[b]])
        down_copy(j).start()

    put_down(down_recv, bag, down_store[slot[bag]])

    loads[2].wait()
    for half in range(2):
        seg = 2 * seq + half
        shift = mod[seg, 0, 0:1, :]
        scale = 1.0 + mod[seg, 0, 1:2, :]

        @pl.loop(0, TEXT // 16)
        def _(i):
            values = normed(text_raw[pl.ds(half * TEXT + i * 16, 16), :].astype(F32))
            text_all[seq, half, pl.ds(i * 16, 16), :] = (scale * values + shift).astype(BF16)


    loads[4].wait()

    @pl.loop(1, bags)
    def _(j):
        b = lax.rem(bag + j, bags)
        up_send[b] = up_store[slot[b]]
        up_copy(j).start()

    up_recv[bag] = up_store[slot[bag]]

    row_ids = iota((1, image_bag), 1)
    segs = jnp.zeros_like(row_ids)
    owners = jnp.zeros_like(row_ids)
    for j in range(2 * users):
        segs = segs + (row_ids >= ends[j]).astype(I32)
    for u in range(users):
        owner = store_row[user_adapter[bag, u]] >> store_bits
        own[u] = owner
        owners = owners + jnp.where(segs >> 1 == u, owner, 0)
    seg_row[...] = segs
    own_r = owners

    def as_column(row):
        wide = jnp.broadcast_to(row.astype(F32), (HEAD_DIM, image_bag))
        return jnp.transpose(wide).astype(I32)

    seg_col[...] = as_column(segs)
    own_col[...] = as_column(owners)

    hop(0, 1)
    hop(0, 2)
    start_own(1, 0)
    start_own(1, 1)
    hop(0, 3)

    def seq_copy(which, j, src, dst):
        return pltpu.make_async_remote_copy(
            src_ref=src,
            dst_ref=dst,
            send_sem=seq_send.at[which, j],
            recv_sem=seq_recv.at[which, j],
            device_id={"seq": lax.rem(seq + j, seqs)},
            device_id_type=MESH,
        )

    def ahead(j):
        return lax.rem(seq + j, seqs)

    def behind(j):
        return lax.rem(seq + seqs - j, seqs)

    def fwd_copy(j):
        return seq_copy(0, j, down_fwd.at[ahead(j)], text_down.at[seq])

    @pl.loop(1, bags)
    def _(j):
        bag_arrival(0, j).wait_recv()

    @pl.loop(1, seqs)
    def _(j):
        u = ahead(j)
        down_fwd[u] = down_recv[own[u], 0]
        fwd_copy(j).start()

    text_down[seq] = down_recv[own[seq], 0]

    hop(1, 1)
    last_hop(0)

    @pl.loop(1, seqs)
    def _(j):
        seq_copy(0, j, down_fwd.at[ahead(j)], text_down.at[behind(j)]).wait_recv()

    parts = 8 * seqs

    def rank_sums(downs, rows_lo, rows_hi):
        low = dot_g(downs, rows_lo, NT)
        high = dot_g(downs, rows_hi, NT)
        first = iota(low.shape, 0) & 7 < 4
        mixed = jnp.where(first, low, high)
        total = mixed + pltpu.roll(mixed, low.shape[0] - 4, 0)
        return total, first

    downs = text_down[...].reshape(parts, depth // 2)
    total, first = rank_sums(
        downs,
        text_all[seq, :, :, : depth // 2].reshape(text_rows, depth // 2),
        text_all[seq, :, :, depth // 2 :].reshape(text_rows, depth // 2),
    )
    sums = jnp.where(first, total, 0.0).astype(BF16)
    at = iota((parts // 2, parts), 0)
    take = (iota((parts // 2, parts), 1) == 8 * (at >> 2) + (at & 3)).astype(BF16)
    rank_all[seq] = dot(take, sums).astype(BF16)

    rank_refs = (None, rank_all, image_rank)

    def core_copy(which, j):
        ref = rank_refs[which].at[seq]
        return pltpu.make_async_remote_copy(
            src_ref=ref,
            dst_ref=ref,
            send_sem=seq_send.at[which, j],
            recv_sem=seq_recv.at[which, j],
            device_id={"seq": slot_of(j, core)},
            device_id_type=MESH,
        )

    def core_arrival(which, j):
        ref = rank_refs[which].at[slot_of(ring - j, core)]
        return pltpu.make_async_remote_copy(
            src_ref=ref,
            dst_ref=ref,
            send_sem=seq_send.at[which, j],
            recv_sem=seq_recv.at[which, j],
            device_id={"seq": mate},
            device_id_type=MESH,
        )

    def pass_copy(which, k, side):
        ref = rank_refs[which].at[slot_of(k, side)]
        return pltpu.make_async_remote_copy(
            src_ref=ref,
            dst_ref=ref,
            send_sem=seq_send.at[which, ring + k],
            recv_sem=seq_recv.at[which, ring + k],
            device_id={"seq": mate},
            device_id_type=MESH,
        )

    def send_ranks(which):
        @pl.loop(1, ring)
        def _(j):
            core_copy(which, j).start()

        pass_copy(which, 0, core).start()

    def take_ranks(which):
        @pl.loop(1, ring)
        def _(j):
            core_arrival(which, j).wait_recv()
            pass_copy(which, ring - j, core).start()

        @pl.loop(0, ring)
        def _(k):
            pass_copy(which, k, 1 - core).wait_recv()

    send_ranks(1)

    @pl.loop(0, ring)
    def _(k):
        for half in range(2):
            mate_copy(0, k, half, 1 - core).wait_recv()

    downs = down_recv[:, 1].reshape(8 * bags, depth // 2)
    total, first = rank_sums(
        downs,
        image_all[:, :, :, : depth // 2].reshape(image_bag, depth // 2),
        image_all[:, :, :, depth // 2 :].reshape(image_bag, depth // 2),
    )
    mine = jnp.logical_and(first, iota(total.shape, 0) >> 3 == own_r)
    sums = jnp.where(mine, total, 0.0).astype(BF16)
    at = iota((8, 8 * bags), 0)
    take = jnp.logical_and(iota(at.shape, 1) & 7 == at, at < 4)
    image_rank[seq] = dot(take.astype(BF16), sums).astype(BF16)

    send_ranks(2)
    hop(1, 2)

    @pl.loop(1, bags)
    def _(j):
        bag_arrival(1, j).wait_recv()

    take_ranks(2)
    loads[5].wait()
    loads[6].wait()
    rank = parts // 2
    up_image = up_recv[:, 1].reshape(bags * rank, 3 * HEAD_DIM)
    rank_bits = rank.bit_length() - 1
    lane = iota((parts, bags * rank), 1) & (rank - 1)
    copies = (iota((parts, bags * rank), 0) == 8 * (lane >> 2) + (lane & 3)).astype(BF16)
    ranks = image_rank[...].reshape(parts, image_bag)
    for lot in range(2):
        lo, rows = lot * image_bag // 2, image_bag // 2
        spread = dot_g(ranks[:, lo : lo + rows], copies, TN)
        here = iota(spread.shape, 1) >> rank_bits == own_col[lo : lo + rows, 0:1]
        spread = jnp.where(here, spread, 0.0).astype(BF16)
        lot_rows = image_all[lot * seqs // 2 : (lot + 1) * seqs // 2].reshape(rows, depth)
        mixed = dot(lot_rows, weight[1]) + dot(spread, up_image)
        query_image[lo : lo + rows] = head_normed(mixed[:, :HEAD_DIM], gain[1, 0:1])
        key_image[lo : lo + rows] = head_normed(
            mixed[:, HEAD_DIM : 2 * HEAD_DIM], gain[1, 1:2]
        )
        value_image[lo : lo + rows] = mixed[:, 2 * HEAD_DIM :].astype(BF16)

    hop(1, 3)
    take_ranks(1)

    group = 4

    def text_out_copy(j):
        return pltpu.make_async_remote_copy(
            src_ref=text_stage.at[ahead(j)],
            dst_ref=text_out.at[seq],
            send_sem=seq_send.at[3, j],
            recv_sem=seq_recv.at[3, j],
            device_id={"seq": ahead(j)},
            device_id_type=MESH,
        )

    def image_out_copy(j):
        return pltpu.make_async_remote_copy(
            src_ref=image_stage.at[ahead(j)],
            dst_ref=image_out.at[seq],
            send_sem=seq_send.at[4, j],
            recv_sem=seq_recv.at[4, j],
            device_id={"seq": ahead(j)},
            device_id_type=MESH,
        )

    text_local = pltpu.make_async_copy(text_stage.at[seq], text_out.at[seq], local_sem.at[7])
    image_local = pltpu.make_async_copy(image_stage.at[seq], image_out.at[seq], local_sem.at[8])

    last_hop(1)

    @pl.loop(0, ring)
    def _(k):
        for half in range(2):
            mate_copy(1, k, half, 1 - core).wait_recv()

    @pl.loop(0, seqs // group)
    def _(p):
        first = group * lax.rem(seq // group + p, seqs // group)
        rows = text_all[pl.ds(first, group)].reshape(group * text_rows, depth)
        plain = dot(rows, weight[0])
        image_segs = seg_row[...]
        for which in range(group):
            u = first + which
            j = lax.rem(seq + seqs - u, seqs)

            adjust = dot_g(rank_all[u], up_recv[own[u], 0], TN)
            mixed = plain[which * text_rows : (which + 1) * text_rows] + adjust
            query = head_normed(mixed[:, :HEAD_DIM], gain[0, 0:1])
            key = head_normed(mixed[:, HEAD_DIM : 2 * HEAD_DIM], gain[0, 1:2])
            value = mixed[:, 2 * HEAD_DIM :].astype(BF16)
            key_text[u] = key
            value_text[u] = value
            near = dot_g(query, key, NT) * factor
            same = iota(near.shape, 0) >> 6 == iota(near.shape, 1) >> 6
            near = jnp.where(same, near, NEG)
            far = dot_g(query, key_image[...], NT) * factor
            same = 2 * u + (iota(far.shape, 0) >> 6) == image_segs
            far = jnp.where(same, far, NEG)
            top = jnp.maximum(
                jnp.max(near, axis=1, keepdims=True), jnp.max(far, axis=1, keepdims=True)
            )
            near = jnp.exp(near - top)
            far = jnp.exp(far - top)
            total = jnp.sum(near, axis=1, keepdims=True) + jnp.sum(far, axis=1, keepdims=True)
            result = dot((near / total).astype(BF16), value) + dot(
                (far / total).astype(BF16), value_image[...]
            )
            text_stage[u] = result.astype(BF16)

            @pl.when(j != 0)
            def _():
                text_out_copy(lax.rem(u + seqs - seq, seqs)).start()

            @pl.when(j == 0)
            def _():
                text_local.start()

    keys = key_text[...].reshape(seqs * text_rows, HEAD_DIM)
    values = value_text[...].reshape(seqs * text_rows, HEAD_DIM)

    @pl.loop(0, image_bag // HEAD_DIM)
    def _(lot):
        part = pl.ds(lot * HEAD_DIM, HEAD_DIM)
        query = query_image[part, :]
        segs = seg_col[part, 0:1]
        near = dot_g(query, key_image[...], NT) * factor
        near = jnp.where(segs == seg_row[...], near, NEG)
        far = dot_g(query, keys, NT) * factor
        far = jnp.where(segs == iota(far.shape, 1) >> 6, far, NEG)
        top = jnp.maximum(
            jnp.max(near, axis=1, keepdims=True), jnp.max(far, axis=1, keepdims=True)
        )
        near = jnp.exp(near - top)
        far = jnp.exp(far - top)
        total = jnp.sum(near, axis=1, keepdims=True) + jnp.sum(far, axis=1, keepdims=True)
        result = dot((near / total).astype(BF16), value_image[...]) + dot(
            (far / total).astype(BF16), values
        )
        per = HEAD_DIM // image_rows
        image_stage[pl.ds(lot * per, per)] = result.astype(BF16).reshape(
            per, image_rows, HEAD_DIM
        )

    image_local.start()

    @pl.loop(1, seqs)
    def _(j):
        image_out_copy(j).start()

    text_local.wait()
    image_local.wait()

    @pl.loop(1, seqs)
    def _(j):
        seq_copy(3, j, text_stage.at[seq], text_out.at[behind(j)]).wait_recv()
        seq_copy(4, j, image_stage.at[seq], image_out.at[behind(j)]).wait_recv()
        fwd_copy(j).wait_send()
        text_out_copy(j).wait_send()
        image_out_copy(j).wait_send()

    for which in (1, 2):

        @pl.loop(1, ring)
        def _(j):
            core_copy(which, j).wait_send()

        @pl.loop(0, ring)
        def _(k):
            pass_copy(which, k, core).wait_send()

    @pl.loop(1, bags)
    def _(j):
        down_copy(j).wait_send()
        up_copy(j).wait_send()

    @pl.loop(0, ring)
    def _(k):
        for st in range(2):
            for half in range(2):
                mate_copy(st, k, half, core).wait_send()

    @pl.loop(0, half_ring - 1)
    def _(h):
        for st in range(2):
            for half in range(2):
                ring_copy(st, 0, lax.rem(ring - h, ring), half).wait_send()
                ring_copy(st, 1, h, half).wait_send()

    for st in range(2):
        ring_copy(st, 0, half_ring + 1, 0).wait_send()
        ring_copy(st, 1, half_ring - 1, 1).wait_send()


def body(
    bags,
    seqs,
    text_rows,
    image_rows,
    modulation,
    head_weight,
    norm_gain,
    store_down,
    store_up,
    store_row,
    user_adapter,
    image_lengths,
):
    ring = seqs // 2
    text_dev, depth = text_rows.shape
    image_dev = image_rows.shape[0]
    image_bag = image_dev * seqs
    store_size = store_down.shape[0]
    rank, width = store_up.shape[2:]
    heads = seqs * HEAD_DIM
    smem = pl.BlockSpec(memory_space=pltpu.SMEM)
    hbm = pl.BlockSpec(memory_space=pl.ANY)
    vmem = pltpu.VMEM
    dma = pltpu.SemaphoreType.DMA
    text_heads, image_heads = pl.pallas_call(
        functools.partial(kernel, bags, ring, store_size),
        out_shape=(
            jax.ShapeDtypeStruct((seqs, text_dev, HEAD_DIM), BF16),
            jax.ShapeDtypeStruct((seqs, image_dev, HEAD_DIM), BF16),
        ),
        in_specs=[smem] * 3 + [hbm] * 7,
        out_specs=(hbm, hbm),
        scratch_shapes=[
            pltpu.SMEM((seqs,), I32),
            pltpu.SMEM((bags,), I32),
            pltpu.SMEM((2 * seqs,), I32),
            vmem((text_dev, depth), BF16),
            vmem((image_dev, depth), BF16),
            vmem(modulation.shape, F32),
            vmem(head_weight.shape, BF16),
            vmem(norm_gain.shape, F32),
            vmem(store_down.shape, BF16),
            vmem(store_up.shape, BF16),
            vmem((bags, 2, 8, depth // 2), BF16),
            vmem((bags, 2, rank, width), BF16),
            vmem((bags, 2, 8, depth // 2), BF16),
            vmem((bags, 2, rank, width), BF16),
            vmem((seqs, 8, depth // 2), BF16),
            vmem((seqs, 8, depth // 2), BF16),
            vmem((2, image_dev, depth), F32),
            vmem((seqs, 2, text_dev // 2, depth), BF16),
            vmem((seqs, 2, image_dev // 2, depth), BF16),
            vmem((seqs, rank, text_dev), BF16),
            vmem((seqs, 8, image_bag), BF16),
            vmem((1, image_bag), I32),
            vmem((image_bag, HEAD_DIM), I32),
            vmem((image_bag, HEAD_DIM), I32),
            vmem((image_bag, HEAD_DIM), BF16),
            vmem((image_bag, HEAD_DIM), BF16),
            vmem((image_bag, HEAD_DIM), BF16),
            vmem((seqs, text_dev, HEAD_DIM), BF16),
            vmem((seqs, text_dev, HEAD_DIM), BF16),
            vmem((seqs, text_dev, HEAD_DIM), BF16),
            vmem((seqs, image_dev, HEAD_DIM), BF16),
            dma((9,)),
            dma((2, bags)),
            dma((2, bags)),
            dma((5, seqs)),
            dma((5, seqs)),
            dma((2, 2, ring, 2)),
            dma((2, ring, 2)),
            dma((2, ring, 2)),
            dma((2, ring, 2)),
        ],
        compiler_params=pltpu.CompilerParams(
            collective_id=0, has_side_effects=True, vmem_limit_bytes=58 * 2**20
        ),
    )(
        user_adapter,
        store_row,
        image_lengths,
        text_rows,
        image_rows,
        modulation,
        head_weight,
        norm_gain,
        store_down,
        store_up,
    )
    return (
        jnp.transpose(text_heads, (1, 0, 2)).reshape(text_dev, heads),
        jnp.transpose(image_heads, (1, 0, 2)).reshape(image_dev, heads),
    )


def solution(mesh):
    in_specs = (
        P(("bag", "seq"), None),
        P(("bag", "seq"), None),
        P("bag", None, None, None),
        P(None, None, "seq"),
        P(),
        P("bag", None, "seq", None),
        P("bag", None, None, "seq"),
        P(),
        P(),
        P("bag", None),
    )
    out_specs = (P(("bag", "seq"), None), P(("bag", "seq"), None))
    return jax.shard_map(
        functools.partial(body, mesh.shape["bag"], mesh.shape["seq"]),
        mesh=mesh,
        in_specs=in_specs,
        out_specs=out_specs,
        check_vma=False,
    )
```

```python
import functools
import math

import jax
import jax.numpy as jnp
from jax import lax
from jax.experimental import pallas as pl
from jax.experimental.pallas import tpu as pltpu
from jax.sharding import PartitionSpec as P

MESH = pl.DeviceIdType.MESH
BF16 = jnp.bfloat16
F32 = jnp.float32
I32 = jnp.int32
HEAD_DIM = 128
TEXT = 64
NEG = -1e30
NT = (((1,), (1,)), ((), ()))
TN = (((0,), (0,)), ((), ()))


def iota(shape, axis):
    return lax.broadcasted_iota(I32, shape, axis)


def normed(values):
    centre = values - jnp.mean(values, axis=-1, keepdims=True)
    spread = jnp.mean(centre * centre, axis=-1, keepdims=True)
    return centre * lax.rsqrt(spread + 1e-06)


def head_normed(values, gain_row):
    spread = jnp.mean(values * values, axis=-1, keepdims=True)
    return (values * lax.rsqrt(spread + 1e-06) * gain_row).astype(BF16)


def dot(a, b):
    return jnp.dot(a, b, preferred_element_type=F32)


def dot_g(a, b, dims):
    return lax.dot_general(a, b, dims, preferred_element_type=F32)


def kernel(
    bags,
    ring,
    store_size,
    user_adapter,
    store_row,
    image_lengths,
    text_in,
    image_in,
    mod_in,
    weight_in,
    gain_in,
    down_in,
    up_in,
    text_out,
    image_out,
    own,
    slot,
    ends,
    text_raw,
    image_raw,
    mod,
    weight,
    gain,
    down_store,
    up_store,
    down_send,
    up_send,
    down_recv,
    up_recv,
    down_fwd,
    text_down,
    image_scale,
    text_all,
    image_all,
    rank_all,
    image_rank,
    seg_row,
    seg_col,
    own_col,
    query_image,
    key_image,
    value_image,
    key_text,
    value_text,
    text_stage,
    image_stage,
    local_sem,
    bag_send,
    bag_recv,
    seq_send,
    seq_recv,
    ring_send,
    ring_recv,
    mate_send,
    mate_recv,
):
    seqs = 2 * ring
    half_ring = ring // 2
    users = seqs
    steps = [users >> i for i in range(users.bit_length())]
    store_bits = store_size.bit_length() - 1
    bag = lax.axis_index("bag")
    seq = lax.axis_index("seq")
    z, core = seq // 2, lax.rem(seq, 2)
    mate = z * 2 + 1 - core
    depth = text_raw.shape[1]
    text_rows = text_raw.shape[0]
    image_rows = image_raw.shape[0]
    image_bag = seqs * image_rows
    image_half = image_rows // 2
    factor = math.log2(math.e) / math.sqrt(HEAD_DIM)

    pairs = (
        (image_in, image_raw),
        (mod_in, mod),
        (text_in, text_raw),
        (down_in, down_store),
        (up_in, up_store),
        (gain_in, gain),
        (weight_in, weight),
    )
    loads = [
        pltpu.make_async_copy(src, dst, local_sem.at[i]) for i, (src, dst) in enumerate(pairs)
    ]
    for load in loads:
        load.start()

    barrier = pltpu.get_barrier_semaphore()

    @pl.loop(1, seqs)
    def _(j):
        pl.semaphore_signal(
            barrier, inc=1, device_id={"seq": lax.rem(seq + j, seqs)}, device_id_type=MESH
        )

    @pl.loop(1, bags)
    def _(j):
        pl.semaphore_signal(
            barrier, inc=1, device_id={"bag": lax.rem(bag + j, bags)}, device_id_type=MESH
        )

    before = jnp.int32(0)
    for u in range(users):
        length = image_lengths[0, u]
        ends[2 * u] = before + length
        before = before + 2 * length
        ends[2 * u + 1] = before

    loads[0].wait()
    loads[1].wait()

    @pl.loop(0, image_rows)
    def _(i):
        row = seq * image_rows + i
        seg = jnp.int32(0)
        for step in steps:
            seg = seg + jnp.where(row >= ends[seg + step - 1], step, 0)
        image_scale[0, pl.ds(i, 1), :] = mod[seg, 1, 0:1, :]
        image_scale[1, pl.ds(i, 1), :] = mod[seg, 1, 1:2, :]

    for half in range(2):
        part = pl.ds(half * image_half, image_half)
        values = normed(image_raw[part, :].astype(F32))
        image_all[seq, half] = (
            (1.0 + image_scale[1, part, :]) * values + image_scale[0, part, :]
        ).astype(BF16)

    pl.semaphore_wait(barrier, seqs - 1 + bags - 1)

    blocks = (image_all, text_all)

    def slot_of(k, which):
        return lax.rem(z + k, ring) * 2 + which

    def ring_copy(st, d, k, half):
        chunk = blocks[st].at[slot_of(k, core), half]
        turn = ring - 1 if d == 0 else 1
        peer = lax.rem(z + (1 if d == 0 else ring - 1), ring) * 2 + core
        return pltpu.make_async_remote_copy(
            src_ref=chunk,
            dst_ref=chunk,
            send_sem=ring_send.at[st, d, k, half],
            recv_sem=ring_recv.at[st, lax.rem(k + turn, ring), half],
            device_id={"seq": peer},
            device_id_type=MESH,
        )

    def ring_arrival(st, k, half):
        chunk = blocks[st].at[slot_of(k, core), half]
        return pltpu.make_async_remote_copy(
            src_ref=chunk,
            dst_ref=chunk,
            send_sem=ring_send.at[st, 0, k, half],
            recv_sem=ring_recv.at[st, k, half],
            device_id={"seq": mate},
            device_id_type=MESH,
        )

    def mate_copy(st, k, half, which):
        chunk = blocks[st].at[slot_of(k, which), half]
        return pltpu.make_async_remote_copy(
            src_ref=chunk,
            dst_ref=chunk,
            send_sem=mate_send.at[st, k, half],
            recv_sem=mate_recv.at[st, k, half],
            device_id={"seq": mate},
            device_id_type=MESH,
        )

    def start_own(st, half):
        ring_copy(st, half, 0, half).start()
        ring_copy(st, 1 - half, 0, half).start()
        mate_copy(st, 0, half, core).start()

    def hop(st, h):
        for d, half in ((0, 0), (1, 1), (0, 1), (1, 0)):
            k = ring - h if d == 0 else h
            ring_arrival(st, k, half).wait_recv()
            if d == half:
                ring_copy(st, d, k, half).start()
            elif h < half_ring - 1:
                ring_copy(st, d, k, half).start()

            mate_copy(st, k, half, core).start()

    def last_hop(st):
        for half in range(2):
            ring_arrival(st, half_ring, half).wait_recv()
            mate_copy(st, half_ring, half, core).start()

    start_own(0, 0)
    start_own(0, 1)

    def down_copy(j):
        b = lax.rem(bag + j, bags)
        return pltpu.make_async_remote_copy(
            src_ref=down_send.at[b],
            dst_ref=down_recv.at[bag],
            send_sem=bag_send.at[0, j],
            recv_sem=bag_recv.at[0, j],
            device_id={"bag": b},
            device_id_type=MESH,
        )

    def up_copy(j):
        b = lax.rem(bag + j, bags)
        return pltpu.make_async_remote_copy(
            src_ref=up_send.at[b],
            dst_ref=up_recv.at[bag],
            send_sem=bag_send.at[1, j],
            recv_sem=bag_recv.at[1, j],
            device_id={"bag": b},
            device_id_type=MESH,
        )

    def bag_arrival(which, j):
        ref = (down_recv, up_recv)[which].at[lax.rem(bag + bags - j, bags)]
        return pltpu.make_async_remote_copy(
            src_ref=ref,
            dst_ref=ref,
            send_sem=bag_send.at[which, j],
            recv_sem=bag_recv.at[which, j],
            device_id={"bag": lax.rem(bag + j, bags)},
            device_id_type=MESH,
        )

    @pl.loop(0, bags)
    def _(b):
        total = jnp.int32(0)
        for u in range(users):
            row = store_row[user_adapter[b, u]]
            total = total + jnp.where(row >> store_bits == bag, row & (store_size - 1), 0)
        slot[b] = total

    loads[3].wait()

    def put_down(ref, index, block):
        ref[index, :, 0:4, :] = block[:, :, : depth // 2]
        ref[index, :, 4:8, :] = block[:, :, depth // 2 :]

    @pl.loop(1, bags)
    def _(j):
        b = lax.rem(bag + j, bags)
        put_down(down_send, b, down_store[slot[b]])
        down_copy(j).start()

    put_down(down_recv, bag, down_store[slot[bag]])

    loads[2].wait()
    for half in range(2):
        seg = 2 * seq + half
        shift = mod[seg, 0, 0:1, :]
        scale = 1.0 + mod[seg, 0, 1:2, :]

        @pl.loop(0, TEXT // 16)
        def _(i):
            values = normed(text_raw[pl.ds(half * TEXT + i * 16, 16), :].astype(F32))
            text_all[seq, half, pl.ds(i * 16, 16), :] = (scale * values + shift).astype(BF16)


    loads[4].wait()

    @pl.loop(1, bags)
    def _(j):
        b = lax.rem(bag + j, bags)
        up_send[b] = up_store[slot[b]]
        up_copy(j).start()

    up_recv[bag] = up_store[slot[bag]]

    row_ids = iota((1, image_bag), 1)
    segs = jnp.zeros_like(row_ids)
    owners = jnp.zeros_like(row_ids)
    for j in range(2 * users):
        segs = segs + (row_ids >= ends[j]).astype(I32)
    for u in range(users):
        owner = store_row[user_adapter[bag, u]] >> store_bits
        own[u] = owner
        owners = owners + jnp.where(segs >> 1 == u, owner, 0)
    seg_row[...] = segs
    own_r = owners

    def as_column(row):
        wide = jnp.broadcast_to(row.astype(F32), (HEAD_DIM, image_bag))
        return jnp.transpose(wide).astype(I32)

    seg_col[...] = as_column(segs)
    own_col[...] = as_column(owners)

    hop(0, 1)
    hop(0, 2)
    start_own(1, 0)
    start_own(1, 1)
    hop(0, 3)

    def seq_copy(which, j, src, dst):
        return pltpu.make_async_remote_copy(
            src_ref=src,
            dst_ref=dst,
            send_sem=seq_send.at[which, j],
            recv_sem=seq_recv.at[which, j],
            device_id={"seq": lax.rem(seq + j, seqs)},
            device_id_type=MESH,
        )

    def ahead(j):
        return lax.rem(seq + j, seqs)

    def behind(j):
        return lax.rem(seq + seqs - j, seqs)

    def fwd_copy(j):
        return seq_copy(0, j, down_fwd.at[ahead(j)], text_down.at[seq])

    @pl.loop(1, bags)
    def _(j):
        bag_arrival(0, j).wait_recv()

    @pl.loop(1, seqs)
    def _(j):
        u = ahead(j)
        down_fwd[u] = down_recv[own[u], 0]
        fwd_copy(j).start()

    text_down[seq] = down_recv[own[seq], 0]

    hop(1, 1)
    last_hop(0)

    @pl.loop(1, seqs)
    def _(j):
        seq_copy(0, j, down_fwd.at[ahead(j)], text_down.at[behind(j)]).wait_recv()

    parts = 8 * seqs

    def rank_sums(downs, rows_lo, rows_hi):
        low = dot_g(downs, rows_lo, NT)
        high = dot_g(downs, rows_hi, NT)
        first = iota(low.shape, 0) & 7 < 4
        mixed = jnp.where(first, low, high)
        total = mixed + pltpu.roll(mixed, low.shape[0] - 4, 0)
        return total, first

    downs = text_down[...].reshape(parts, depth // 2)
    total, first = rank_sums(
        downs,
        text_all[seq, :, :, : depth // 2].reshape(text_rows, depth // 2),
        text_all[seq, :, :, depth // 2 :].reshape(text_rows, depth // 2),
    )
    sums = jnp.where(first, total, 0.0).astype(BF16)
    at = iota((parts // 2, parts), 0)
    take = (iota((parts // 2, parts), 1) == 8 * (at >> 2) + (at & 3)).astype(BF16)
    rank_all[seq] = dot(take, sums).astype(BF16)

    rank_refs = (None, rank_all, image_rank)

    def core_copy(which, j):
        ref = rank_refs[which].at[seq]
        return pltpu.make_async_remote_copy(
            src_ref=ref,
            dst_ref=ref,
            send_sem=seq_send.at[which, j],
            recv_sem=seq_recv.at[which, j],
            device_id={"seq": slot_of(j, core)},
            device_id_type=MESH,
        )

    def core_arrival(which, j):
        ref = rank_refs[which].at[slot_of(ring - j, core)]
        return pltpu.make_async_remote_copy(
            src_ref=ref,
            dst_ref=ref,
            send_sem=seq_send.at[which, j],
            recv_sem=seq_recv.at[which, j],
            device_id={"seq": mate},
            device_id_type=MESH,
        )

    def pass_copy(which, k, side):
        ref = rank_refs[which].at[slot_of(k, side)]
        return pltpu.make_async_remote_copy(
            src_ref=ref,
            dst_ref=ref,
            send_sem=seq_send.at[which, ring + k],
            recv_sem=seq_recv.at[which, ring + k],
            device_id={"seq": mate},
            device_id_type=MESH,
        )

    def send_ranks(which):
        @pl.loop(1, ring)
        def _(j):
            core_copy(which, j).start()

        pass_copy(which, 0, core).start()

    def take_ranks(which):
        @pl.loop(1, ring)
        def _(j):
            core_arrival(which, j).wait_recv()
            pass_copy(which, ring - j, core).start()

        @pl.loop(0, ring)
        def _(k):
            pass_copy(which, k, 1 - core).wait_recv()

    send_ranks(1)

    @pl.loop(0, ring)
    def _(k):
        for half in range(2):
            mate_copy(0, k, half, 1 - core).wait_recv()

    downs = down_recv[:, 1].reshape(8 * bags, depth // 2)
    total, first = rank_sums(
        downs,
        image_all[:, :, :, : depth // 2].reshape(image_bag, depth // 2),
        image_all[:, :, :, depth // 2 :].reshape(image_bag, depth // 2),
    )
    mine = jnp.logical_and(first, iota(total.shape, 0) >> 3 == own_r)
    sums = jnp.where(mine, total, 0.0).astype(BF16)
    at = iota((8, 8 * bags), 0)
    take = jnp.logical_and(iota(at.shape, 1) & 7 == at, at < 4)
    image_rank[seq] = dot(take.astype(BF16), sums).astype(BF16)

    send_ranks(2)
    hop(1, 2)
    hop(1, 3)

    @pl.loop(1, bags)
    def _(j):
        bag_arrival(1, j).wait_recv()

    take_ranks(2)
    loads[5].wait()
    loads[6].wait()
    rank = parts // 2
    up_image = up_recv[:, 1].reshape(bags * rank, 3 * HEAD_DIM)
    rank_bits = rank.bit_length() - 1
    lane = iota((parts, bags * rank), 1) & (rank - 1)
    copies = (iota((parts, bags * rank), 0) == 8 * (lane >> 2) + (lane & 3)).astype(BF16)
    ranks = image_rank[...].reshape(parts, image_bag)
    for lot in range(2):
        lo, rows = lot * image_bag // 2, image_bag // 2
        spread = dot_g(ranks[:, lo : lo + rows], copies, TN)
        here = iota(spread.shape, 1) >> rank_bits == own_col[lo : lo + rows, 0:1]
        spread = jnp.where(here, spread, 0.0).astype(BF16)
        lot_rows = image_all[lot * seqs // 2 : (lot + 1) * seqs // 2].reshape(rows, depth)
        mixed = dot(lot_rows, weight[1]) + dot(spread, up_image)
        query_image[lo : lo + rows] = head_normed(mixed[:, :HEAD_DIM], gain[1, 0:1])
        key_image[lo : lo + rows] = head_normed(
            mixed[:, HEAD_DIM : 2 * HEAD_DIM], gain[1, 1:2]
        )
        value_image[lo : lo + rows] = mixed[:, 2 * HEAD_DIM :].astype(BF16)

    take_ranks(1)

    group = 4

    def text_out_copy(j):
        return pltpu.make_async_remote_copy(
            src_ref=text_stage.at[ahead(j)],
            dst_ref=text_out.at[seq],
            send_sem=seq_send.at[3, j],
            recv_sem=seq_recv.at[3, j],
            device_id={"seq": ahead(j)},
            device_id_type=MESH,
        )

    def image_out_copy(j):
        return pltpu.make_async_remote_copy(
            src_ref=image_stage.at[ahead(j)],
            dst_ref=image_out.at[seq],
            send_sem=seq_send.at[4, j],
            recv_sem=seq_recv.at[4, j],
            device_id={"seq": ahead(j)},
            device_id_type=MESH,
        )

    text_local = pltpu.make_async_copy(text_stage.at[seq], text_out.at[seq], local_sem.at[7])
    image_local = pltpu.make_async_copy(image_stage.at[seq], image_out.at[seq], local_sem.at[8])

    last_hop(1)

    @pl.loop(0, ring)
    def _(k):
        for half in range(2):
            mate_copy(1, k, half, 1 - core).wait_recv()

    @pl.loop(0, seqs // group)
    def _(p):
        first = group * lax.rem(seq // group + p, seqs // group)
        rows = text_all[pl.ds(first, group)].reshape(group * text_rows, depth)
        plain = dot(rows, weight[0])
        image_segs = seg_row[...]
        for which in range(group):
            u = first + which
            j = lax.rem(seq + seqs - u, seqs)

            adjust = dot_g(rank_all[u], up_recv[own[u], 0], TN)
            mixed = plain[which * text_rows : (which + 1) * text_rows] + adjust
            query = head_normed(mixed[:, :HEAD_DIM], gain[0, 0:1])
            key = head_normed(mixed[:, HEAD_DIM : 2 * HEAD_DIM], gain[0, 1:2])
            value = mixed[:, 2 * HEAD_DIM :].astype(BF16)
            key_text[u] = key
            value_text[u] = value
            near = dot_g(query, key, NT)
            same = iota(near.shape, 0) >> 6 == iota(near.shape, 1) >> 6
            near = jnp.where(same, near, NEG)
            far = dot_g(query, key_image[...], NT)
            same = 2 * u + (iota(far.shape, 0) >> 6) == image_segs
            far = jnp.where(same, far, NEG)
            top = jnp.maximum(
                jnp.max(near, axis=1, keepdims=True), jnp.max(far, axis=1, keepdims=True)
            )
            near = jnp.exp2((near - top) * factor)
            far = jnp.exp2((far - top) * factor)
            total = jnp.sum(near, axis=1, keepdims=True) + jnp.sum(far, axis=1, keepdims=True)
            total = 1.0 / total
            result = dot((near * total).astype(BF16), value) + dot(
                (far * total).astype(BF16), value_image[...]
            )
            text_stage[u] = result.astype(BF16)

            @pl.when(j != 0)
            def _():
                text_out_copy(lax.rem(u + seqs - seq, seqs)).start()

            @pl.when(j == 0)
            def _():
                text_local.start()

    keys = key_text[...].reshape(seqs * text_rows, HEAD_DIM)
    values = value_text[...].reshape(seqs * text_rows, HEAD_DIM)

    @pl.loop(0, image_bag // HEAD_DIM)
    def _(lot):
        part = pl.ds(lot * HEAD_DIM, HEAD_DIM)
        query = query_image[part, :]
        segs = seg_col[part, 0:1]
        near = dot_g(query, key_image[...], NT)
        near = jnp.where(segs == seg_row[...], near, NEG)
        far = dot_g(query, keys, NT)
        far = jnp.where(segs == iota(far.shape, 1) >> 6, far, NEG)
        top = jnp.maximum(
            jnp.max(near, axis=1, keepdims=True), jnp.max(far, axis=1, keepdims=True)
        )
        near = jnp.exp2((near - top) * factor)
        far = jnp.exp2((far - top) * factor)
        total = jnp.sum(near, axis=1, keepdims=True) + jnp.sum(far, axis=1, keepdims=True)
        total = 1.0 / total
        result = dot((near * total).astype(BF16), value_image[...]) + dot(
            (far * total).astype(BF16), values
        )
        per = HEAD_DIM // image_rows
        image_stage[pl.ds(lot * per, per)] = result.astype(BF16).reshape(
            per, image_rows, HEAD_DIM
        )

    image_local.start()

    @pl.loop(1, seqs)
    def _(j):
        image_out_copy(j).start()

    text_local.wait()
    image_local.wait()

    @pl.loop(1, seqs)
    def _(j):
        seq_copy(3, j, text_stage.at[seq], text_out.at[behind(j)]).wait_recv()
        seq_copy(4, j, image_stage.at[seq], image_out.at[behind(j)]).wait_recv()
        fwd_copy(j).wait_send()
        text_out_copy(j).wait_send()
        image_out_copy(j).wait_send()

    for which in (1, 2):

        @pl.loop(1, ring)
        def _(j):
            core_copy(which, j).wait_send()

        @pl.loop(0, ring)
        def _(k):
            pass_copy(which, k, core).wait_send()

    @pl.loop(1, bags)
    def _(j):
        down_copy(j).wait_send()
        up_copy(j).wait_send()

    @pl.loop(0, ring)
    def _(k):
        for st in range(2):
            for half in range(2):
                mate_copy(st, k, half, core).wait_send()

    @pl.loop(0, half_ring - 1)
    def _(h):
        for st in range(2):
            for half in range(2):
                ring_copy(st, 0, lax.rem(ring - h, ring), half).wait_send()
                ring_copy(st, 1, h, half).wait_send()

    for st in range(2):
        ring_copy(st, 0, half_ring + 1, 0).wait_send()
        ring_copy(st, 1, half_ring - 1, 1).wait_send()


def body(
    bags,
    seqs,
    text_rows,
    image_rows,
    modulation,
    head_weight,
    norm_gain,
    store_down,
    store_up,
    store_row,
    user_adapter,
    image_lengths,
):
    ring = seqs // 2
    text_dev, depth = text_rows.shape
    image_dev = image_rows.shape[0]
    image_bag = image_dev * seqs
    store_size = store_down.shape[0]
    rank, width = store_up.shape[2:]
    heads = seqs * HEAD_DIM
    smem = pl.BlockSpec(memory_space=pltpu.SMEM)
    hbm = pl.BlockSpec(memory_space=pl.ANY)
    vmem = pltpu.VMEM
    dma = pltpu.SemaphoreType.DMA
    text_heads, image_heads = pl.pallas_call(
        functools.partial(kernel, bags, ring, store_size),
        out_shape=(
            jax.ShapeDtypeStruct((seqs, text_dev, HEAD_DIM), BF16),
            jax.ShapeDtypeStruct((seqs, image_dev, HEAD_DIM), BF16),
        ),
        in_specs=[smem] * 3 + [hbm] * 7,
        out_specs=(hbm, hbm),
        scratch_shapes=[
            pltpu.SMEM((seqs,), I32),
            pltpu.SMEM((bags,), I32),
            pltpu.SMEM((2 * seqs,), I32),
            vmem((text_dev, depth), BF16),
            vmem((image_dev, depth), BF16),
            vmem(modulation.shape, F32),
            vmem(head_weight.shape, BF16),
            vmem(norm_gain.shape, F32),
            vmem(store_down.shape, BF16),
            vmem(store_up.shape, BF16),
            vmem((bags, 2, 8, depth // 2), BF16),
            vmem((bags, 2, rank, width), BF16),
            vmem((bags, 2, 8, depth // 2), BF16),
            vmem((bags, 2, rank, width), BF16),
            vmem((seqs, 8, depth // 2), BF16),
            vmem((seqs, 8, depth // 2), BF16),
            vmem((2, image_dev, depth), F32),
            vmem((seqs, 2, text_dev // 2, depth), BF16),
            vmem((seqs, 2, image_dev // 2, depth), BF16),
            vmem((seqs, rank, text_dev), BF16),
            vmem((seqs, 8, image_bag), BF16),
            vmem((1, image_bag), I32),
            vmem((image_bag, HEAD_DIM), I32),
            vmem((image_bag, HEAD_DIM), I32),
            vmem((image_bag, HEAD_DIM), BF16),
            vmem((image_bag, HEAD_DIM), BF16),
            vmem((image_bag, HEAD_DIM), BF16),
            vmem((seqs, text_dev, HEAD_DIM), BF16),
            vmem((seqs, text_dev, HEAD_DIM), BF16),
            vmem((seqs, text_dev, HEAD_DIM), BF16),
            vmem((seqs, image_dev, HEAD_DIM), BF16),
            dma((9,)),
            dma((2, bags)),
            dma((2, bags)),
            dma((5, seqs)),
            dma((5, seqs)),
            dma((2, 2, ring, 2)),
            dma((2, ring, 2)),
            dma((2, ring, 2)),
            dma((2, ring, 2)),
        ],
        compiler_params=pltpu.CompilerParams(
            collective_id=0, has_side_effects=True, vmem_limit_bytes=58 * 2**20
        ),
    )(
        user_adapter,
        store_row,
        image_lengths,
        text_rows,
        image_rows,
        modulation,
        head_weight,
        norm_gain,
        store_down,
        store_up,
    )
    return (
        jnp.transpose(text_heads, (1, 0, 2)).reshape(text_dev, heads),
        jnp.transpose(image_heads, (1, 0, 2)).reshape(image_dev, heads),
    )


def solution(mesh):
    in_specs = (
        P(("bag", "seq"), None),
        P(("bag", "seq"), None),
        P("bag", None, None, None),
        P(None, None, "seq"),
        P(),
        P("bag", None, "seq", None),
        P("bag", None, None, "seq"),
        P(),
        P(),
        P("bag", None),
    )
    out_specs = (P(("bag", "seq"), None), P(("bag", "seq"), None))
    return jax.shard_map(
        functools.partial(body, mesh.shape["bag"], mesh.shape["seq"]),
        mesh=mesh,
        in_specs=in_specs,
        out_specs=out_specs,
        check_vma=False,
    )
```
